128 devices in a mesh: row: 16 (over x, z_hi, core), col: 8 (over z_lo, y).
Axes of the slice: x: 4, y: 4, z: 4 (z_hi: 2, z_lo: 2; z = z_hi * 2 + z_lo), core: 2. Of those that a mesh axis runs over, the one named last changes fastest.
Arguments:
- thin_line_values: float32 [2048, 65536], P('row', 'col'), may hold values from 0 to 65520, as said below
- occupied_patch_flags: int32 [16, 512], P('row', 'col'), may hold values 0 or 1
- leader_vertical_patch: int32 [2], replicated, may hold values from 0 to 511, as said below
- leader_square_lines: float32 [2, 128, 65536], P(None, 'row', 'col'), may hold values from 0 to 65520, as said below
- leader_square_reciprocals: float32 [2, 128, 128], replicated, may hold values from 0 to 65520, as said below
- remaining_destination_line: int32 [2048], P('row'), may hold values from 0 to 15, as said below
- leading_square_lines: float32 [512, 65536], P('row', 'col'), may hold values from 0 to 65520, as said below
- leading_square_reciprocal: float32 [512, 512], replicated, may hold values from 0 to 65520, as said below
Outputs:
- dense_grid: float32 [4096, 65536], P('row', 'col')
The draws below stay inside these ranges and needn't reach their ends.
Inputs may be any that keep to these rules, and one draw needn't show every extreme that they name: `leader_vertical_patch`: distinct column tiles; the last column tile is among them. `remaining_destination_line`: among the rows of one index of row no value appears more than 16 times; one value, the same for every index of row, appears exactly 16 times in each. `thin_line_values`: Integers. `leader_square_lines`: Integers. `leader_square_reciprocals`: Integers. `leading_square_lines`: Integers. `leading_square_reciprocal`: Integers.
All inputs are finite; a program needn't handle non-finite values. No bound on the sum of `occupied_patch_flags` on one device may be relied on, other than what follows from the above.
Results may differ from the reference program's by a relative error of at most 0.0003.
Values sent between devices are 32-bit elements; how exact they have to be, the bound alone decides.
A program may use at most 256 MiB of HBM per device.

```python
import jax
import jax.numpy as jnp
from jax import lax

TILE = 128
PANEL = 512
WIN = 65536
NPIV = 2
THIN_LINES_EACH = 128
MAX_PER_DEST = 16
SROWS = 2048
DROWS = 4096
N_ROW = 16
N_COL = 8


def residue_block(key, shape):
    uniform_part = jax.random.uniform(key, shape, jnp.float32)
    values = jnp.minimum(jnp.floor(uniform_part * 65521.0), 65520.0)
    return values


def draw_thin_line_values(key, part):
    return residue_block(jax.random.fold_in(key, 11), (SROWS, WIN))


def draw_leader_square_lines(key, part):
    return residue_block(jax.random.fold_in(key, 12), (NPIV, TILE, WIN))


def draw_leader_square_reciprocals(key, part):
    return residue_block(jax.random.fold_in(key, 13), (NPIV, TILE, TILE))


def draw_leading_square_lines(key, part):
    return residue_block(jax.random.fold_in(key, 14), (PANEL, WIN))


def draw_leading_square_reciprocal(key, part):
    return residue_block(jax.random.fold_in(key, 15), (PANEL, PANEL))


def draw_leader_vertical_patch(key, part):
    shuffled = jax.random.permutation(jax.random.fold_in(key, 16), WIN // TILE - 1).astype(jnp.int32)
    listed = jnp.concatenate([jnp.full((1,), WIN // TILE - 1, jnp.int32), shuffled[:NPIV - 1]])
    return jax.random.permutation(jax.random.fold_in(key, 18), listed).astype(jnp.int32)


def draw_remaining_destination_line(key, part):
    base_key = jax.random.fold_in(key, 17)
    hottest = jax.random.randint(jax.random.fold_in(base_key, 1), (), 0, N_ROW).astype(jnp.int32)
    slot_dest = jnp.repeat(jnp.arange(N_ROW, dtype=jnp.int32), MAX_PER_DEST)

    def sender(sender_index):
        sender_key = jax.random.fold_in(base_key, sender_index + 100)
        shuffled = jax.random.permutation(jax.random.fold_in(sender_key, 1), N_ROW * MAX_PER_DEST).astype(jnp.int32)
        scores = (slot_dest == hottest).astype(jnp.int32) * (N_ROW * MAX_PER_DEST) + shuffled
        order = jnp.argsort(scores)
        chosen = slot_dest[order[:THIN_LINES_EACH - MAX_PER_DEST]]
        whole = jnp.concatenate([jnp.full((MAX_PER_DEST,), hottest, jnp.int32), chosen])
        return jax.random.permutation(jax.random.fold_in(sender_key, 2), whole)
    return jax.vmap(sender)(jnp.arange(N_ROW, dtype=jnp.int32)).reshape(SROWS).astype(jnp.int32)


def set_ends(drawn, own_key, least, largest):
    extent = drawn.shape
    place = [jax.random.randint(jax.random.fold_in(own_key, axis), (), 0, extent[axis]) for axis in range(len(extent))]
    drawn = drawn.at[tuple(place)].set(least)
    longest = extent.index(max(extent))
    place[longest] = (place[longest] + 1) % extent[longest]
    return drawn.at[tuple(place)].set(largest)


def setup_inputs(seed: int = 0) -> dict:
    key_of = jax.random.split(jax.random.key(seed), 9)
    return {
        "thin_line_values": draw_thin_line_values(jax.random.fold_in(key_of[8], 71), 0),
        "occupied_patch_flags": set_ends((jax.random.randint(key_of[1], (SROWS // TILE, WIN // TILE), 0, 2) < 1).astype(jnp.int32), jax.random.fold_in(key_of[1], 1), 0, 1),
        "leader_vertical_patch": draw_leader_vertical_patch(jax.random.fold_in(key_of[8], 71), 0),
        "leader_square_lines": draw_leader_square_lines(jax.random.fold_in(key_of[8], 71), 0),
        "leader_square_reciprocals": draw_leader_square_reciprocals(jax.random.fold_in(key_of[8], 71), 0),
        "remaining_destination_line": draw_remaining_destination_line(jax.random.fold_in(key_of[8], 71), 0),
        "leading_square_lines": draw_leading_square_lines(jax.random.fold_in(key_of[8], 71), 0),
        "leading_square_reciprocal": draw_leading_square_reciprocal(jax.random.fold_in(key_of[8], 71), 0),
    }


modulus = 65521.0


def reduce_mod(values):
    quotient = jnp.floor(values / modulus)
    remain = values - quotient * modulus
    remain = jnp.where(remain < 0.0, remain + modulus, remain)
    return jnp.where(remain >= modulus, remain - modulus, remain)


def split_limbs(values):
    upper = jnp.floor(values / 256.0)
    return upper, values - upper * 256.0


def mat_dot(left, right):
    return jnp.dot(left, right, preferred_element_type=jnp.float32, precision=lax.Precision.HIGHEST)


def mul_mod(left, right):
    left_hi, left_lo = split_limbs(left)
    right_hi, right_lo = split_limbs(right)
    total = jnp.zeros((left.shape[0], right.shape[1]), jnp.float32)
    for offset in range(0, left.shape[1], 128):
        a_hi = left_hi[:, offset:offset + 128]
        a_lo = left_lo[:, offset:offset + 128]
        b_hi = right_hi[offset:offset + 128]
        b_lo = right_lo[offset:offset + 128]
        high = mat_dot(a_hi, b_hi)
        cross = mat_dot(a_hi, b_lo) + mat_dot(a_lo, b_hi)
        low = mat_dot(a_lo, b_lo)
        part = reduce_mod(reduce_mod(cross) * 256.0) + reduce_mod(high) * 15.0 + reduce_mod(low)
        total = reduce_mod(total + part)
    return total


def reference(thin_line_values, occupied_patch_flags, leader_vertical_patch, leader_square_lines, leader_square_reciprocals, remaining_destination_line, leading_square_lines, leading_square_reciprocal):
    pattern = occupied_patch_flags.astype(jnp.float32)

    def masked_columns(begin, width):
        rows_part = lax.dynamic_slice_in_dim(thin_line_values, begin, width, 1)
        tiles_part = lax.dynamic_slice_in_dim(pattern, begin // TILE, width // TILE, 1)
        expanded = jnp.repeat(jnp.repeat(tiles_part, TILE, 0), TILE, 1)
        return rows_part * expanded

    factors = []
    for pivot in range(NPIV):
        column = (leader_vertical_patch[pivot] * TILE).astype(jnp.int32)
        tile_now = masked_columns(column, TILE)
        for earlier in range(pivot):
            prior = lax.dynamic_slice_in_dim(leader_square_lines[earlier], column, TILE, 1)
            tile_now = reduce_mod(tile_now - mul_mod(factors[earlier], prior))
        factors.append(mul_mod(tile_now, leader_square_reciprocals[pivot]))

    bucketed_lines = remaining_destination_line.reshape(N_ROW, THIN_LINES_EACH)
    indicator_matrix = (bucketed_lines[:, :, None] == jnp.arange(N_ROW, dtype=jnp.int32)[None, None, :]).astype(jnp.int32)
    landing_order = jnp.sum((jnp.cumsum(indicator_matrix, axis=1) - 1) * indicator_matrix, axis=2)
    sources = jnp.arange(N_ROW, dtype=jnp.int32)[:, None]
    target = (bucketed_lines * (N_ROW * MAX_PER_DEST) + sources * MAX_PER_DEST + landing_order).reshape(SROWS).astype(jnp.int32)

    def gridded_columns(begin, width):
        eliminated_lines = masked_columns(begin, width)
        for pivot in range(NPIV):
            block = lax.dynamic_slice_in_dim(leader_square_lines[pivot], begin, width, 1)
            eliminated_lines = reduce_mod(eliminated_lines - mul_mod(factors[pivot], block))
        return jnp.zeros((DROWS, width), jnp.float32).at[target].set(eliminated_lines)

    lower = mul_mod(gridded_columns(jnp.int32(0), PANEL), leading_square_reciprocal)
    block_width = WIN // N_COL

    def finish(block_index):
        begin = (block_index * block_width).astype(jnp.int32)
        patchwise_arrangement = gridded_columns(begin, block_width)
        strip = lax.dynamic_slice_in_dim(leading_square_lines, begin, block_width, 1)
        return reduce_mod(patchwise_arrangement - mul_mod(lower, strip)) / modulus

    blocks = lax.map(finish, jnp.arange(N_COL, dtype=jnp.int32))
    return jnp.transpose(blocks, (1, 0, 2)).reshape(DROWS, WIN)
```

```python
import functools

import jax
import jax.numpy as jnp
from jax import lax
from jax.experimental import pallas as pl
from jax.experimental.pallas import tpu as pltpu
from jax.sharding import PartitionSpec as P

TILE = 128
PANEL = 512
SLOTS = 16
MODULUS = 65521.0
INVERSE = 1.0 / 65521.0
MESH = pl.DeviceIdType.MESH
F32, BF16 = jnp.float32, jnp.bfloat16
ANY = pl.BlockSpec(memory_space=pl.ANY)
VM = pl.BlockSpec(memory_space=pltpu.VMEM)
SM = pl.BlockSpec(memory_space=pltpu.SMEM)


def dot(a, b):
    return jnp.dot(a, b, preferred_element_type=F32)


def nearest(values):
    return values - jnp.floor(values * INVERSE + 0.5) * MODULUS


def centred(values):
    return jnp.where(values > 32760.0, values - MODULUS, values)


def limbs(values):
    high = jnp.floor(values * (1.0 / 256.0) + 0.5)
    return high.astype(BF16), (values - high * 256.0).astype(BF16)


def subtract_product(base, left, right):
    (a_hi, a_lo), (b_hi, b_lo) = left, right
    cross = nearest(nearest(dot(a_hi, b_lo)) + dot(a_lo, b_hi))
    upper = nearest(256.0 * cross + 15.0 * nearest(dot(a_hi, b_hi)))
    return nearest(base - upper - dot(a_lo, b_lo))


def bucket_kernel(owned, flags, x_ref, dest_ref, piv_ref, out_ref, tile_ref, panel_ref, pick_ref):
    step = pl.program_id(0)
    block = x_ref.shape[1]
    tiles = block // TILE

    @pl.when(step == 0)
    def _():
        wide = jnp.broadcast_to(dest_ref[...], (TILE, TILE)).astype(F32)
        earlier = lax.broadcasted_iota(jnp.int32, (TILE, TILE), 0) < lax.broadcasted_iota(jnp.int32, (TILE, TILE), 1)
        same = jnp.where(earlier & (wide == wide.T), 1.0, 0.0)
        place = dest_ref[...].astype(F32) * SLOTS + jnp.sum(same, axis=0, keepdims=True)
        slot = lax.broadcasted_iota(jnp.int32, pick_ref.shape, 0).astype(F32)
        pick_ref[...] = jnp.where(slot == place, 1.0, 0.0).astype(BF16)
        tile_ref[...] = jnp.zeros_like(tile_ref)
        for t in range(PANEL // TILE):
            s = pl.ds(t * TILE, TILE)
            panel_ref[pl.ds(0, TILE), s] = x_ref[:, s] * flags[0, t].astype(F32)
        for k in range(2):
            panel_ref[pl.ds(TILE + 8 * k, 8), :] = piv_ref[k, :, :PANEL]

    pick = pick_ref[...]
    for t in range(tiles):
        s = pl.ds(t * TILE, TILE)
        x = x_ref[:, s] * flags[0, step * tiles + t].astype(F32)
        high = jnp.floor(x * (1.0 / 256.0))
        out_ref[:, s] = 256.0 * dot(pick, high.astype(BF16)) + dot(pick, (x - high * 256.0).astype(BF16))

    for k in range(2):
        tile = owned[k]

        @pl.when((tile >= step * tiles) & (tile < (step + 1) * tiles))
        def _():
            s = pl.ds(pl.multiple_of((tile - step * tiles) * TILE, TILE), TILE)
            tile_ref[pl.ds(0, TILE), pl.ds(k * TILE, TILE)] = x_ref[:, s] * flags[0, tile].astype(F32)
            if k == 1:
                tile_ref[pl.ds(TILE, 8), pl.ds(0, TILE)] = piv_ref[0, :, s]


def bucket(owned, flags, x, dest, piv):
    rows, width = x.shape
    block = 1024
    slots = 16 * SLOTS
    return pl.pallas_call(
        bucket_kernel,
        grid=(width // block,),
        in_specs=[
            SM,
            SM,
            pl.BlockSpec((rows, block), lambda i: (0, i)),
            pl.BlockSpec((1, rows), lambda i: (0, 0)),
            pl.BlockSpec((2, 8, block), lambda i: (0, 0, i)),
        ],
        out_specs=[
            pl.BlockSpec((slots, block), lambda i: (0, i)),
            pl.BlockSpec((rows + 8, 2 * TILE), lambda i: (0, 0)),
            pl.BlockSpec((rows + 16, PANEL), lambda i: (0, 0)),
            pl.BlockSpec((slots, rows), lambda i: (0, 0)),
        ],
        out_shape=[
            jax.ShapeDtypeStruct((slots, width), F32),
            jax.ShapeDtypeStruct((rows + 8, 2 * TILE), F32),
            jax.ShapeDtypeStruct((rows + 16, PANEL), F32),
            jax.ShapeDtypeStruct((slots, rows), BF16),
        ],
        name="bucket",
    )(owned, flags, x, dest, piv)


SENDS = [(1, 0, 0), (3, 0, 0), (0, 1, 0), (2, 0, 0), (1, 0, 1), (3, 0, 1), (0, 1, 1), (2, 0, 1),
         (1, 1, 0), (3, 1, 0), (2, 1, 0), (1, 1, 1), (3, 1, 1), (2, 1, 1), (0, 0, 1)]
NCHUNK = 4


def exchange_kernel(
    rows_ref, piv_ref, strip_ref, tile_ref, panel_ref, pick_ref,
    g_ref, ext_ref, pivs_ref, strips_ref, bx_ref,
    ext_out, bx_out, tile_in, panel_in,
    tile_s, tile_r, panel_s, panel_r, row_s, row_r, ext_s, ext_r, ag_s, ag_r, core_r, local_s,
):
    r, c = lax.axis_index("row"), lax.axis_index("col")
    x, h, core = r // 4, lax.rem(r // 2, 2), lax.rem(r, 2)

    def peer(dx, dh, dc):
        return lax.rem(x + dx, 4) * 4 + lax.rem(h + dh, 2) * 2 + lax.rem(core + dc, 2)

    def send(src, dst, ssem, rsem, row, col=c):
        return pltpu.make_async_remote_copy(
            src_ref=src, dst_ref=dst, send_sem=ssem, recv_sem=rsem, device_id=(row, col), device_id_type=MESH
        )

    barrier = pltpu.get_barrier_semaphore()
    for off in SENDS:
        pl.semaphore_signal(barrier, inc=1, device_id=(peer(*off), c), device_id_type=MESH)
    for k in range(1, 8):
        pl.semaphore_signal(barrier, inc=1, device_id=(r, lax.rem(c + k, 8)), device_id_type=MESH)
    pl.semaphore_wait(barrier, len(SENDS) + 7)

    tiles = [
        send(tile_ref, tile_in.at[k - 1], tile_s.at[k - 1], tile_r.at[k - 1], r, lax.rem(c + k, 8))
        for k in range(1, 8)
    ]
    panels = [
        send(panel_ref, panel_in, panel_s.at[k - 1], panel_r, r, k) for k in range(1, 8)
    ]
    for t in tiles:
        t.start()

    @pl.when(c == 0)
    def _():
        for p in panels:
            p.start()

    def slices(j, row):
        if j == 0:
            return piv_ref, pivs_ref.at[:, pl.ds(row * 8, 8)]
        if j == 3:
            return bx_out, bx_ref.at[row]
        half = strip_ref.shape[0] // 2
        return (
            strip_ref.at[pl.ds((j - 1) * half, half)],
            strips_ref.at[pl.ds(row * 2 * half + (j - 1) * half, half)],
        )

    RING = [(3, 0), (1, 0), (0, 1), (2, 0), (3, 1), (1, 1), (2, 1)]
    FROM_LEFT, FROM_RIGHT, FROM_PARTNER, FROM_FAR = 0, 1, 2, 3

    def own_copies(j):
        src, dst = slices(j, r)
        return [
            send(src, dst, ag_s.at[j, 0], ag_r.at[j, FROM_LEFT], peer(1, 0, 0)),
            send(src, dst, ag_s.at[j, 1], ag_r.at[j, FROM_RIGHT], peer(3, 0, 0)),
            send(src, dst, ag_s.at[j, 2], ag_r.at[j, FROM_PARTNER], peer(0, 1, 0)),
            send(src, dst, ag_s.at[j, 3], core_r.at[j, 7], peer(0, 0, 1)),
        ]

    def held(j, k):
        return slices(j, peer(RING[k][0], RING[k][1], 0))[1]

    def arrived(j, k):
        return send(held(j, k), held(j, k), ag_s.at[j, 0], ag_r.at[j, k], peer(0, 0, 1))

    def across(j, k):
        return send(held(j, k), held(j, k), ag_s.at[j, 8 + k], core_r.at[j, k], peer(0, 0, 1))

    def locals_(j):
        src, dst = slices(j, r)
        return pltpu.make_async_copy(src, dst, local_s.at[j])

    def onward_left(j):
        return send(held(j, 0), held(j, 0), ag_s.at[j, 4], ag_r.at[j, FROM_FAR], peer(1, 0, 0))

    def onward_right(j):
        return send(held(j, 1), held(j, 1), ag_s.at[j, 4], ag_r.at[j, FROM_FAR], peer(3, 0, 0))

    def partner_right(j):
        return send(held(j, 2), held(j, 2), ag_s.at[j, 5], ag_r.at[j, 4], peer(1, 0, 0))

    def partner_left(j):
        return send(held(j, 2), held(j, 2), ag_s.at[j, 6], ag_r.at[j, 5], peer(3, 0, 0))

    def far_across(j):
        return send(held(j, 3), held(j, 3), ag_s.at[j, 7], ag_r.at[j, 6], peer(0, 1, 0))

    def forward(j):
        odd = lax.rem(x + j, 2) == 1
        arrived(j, 0).wait_recv()
        pl.when(odd)(lambda: onward_left(j).start())
        across(j, 0).start()
        arrived(j, 1).wait_recv()
        pl.when(jnp.logical_not(odd))(lambda: onward_right(j).start())
        across(j, 1).start()
        arrived(j, 2).wait_recv()
        partner_right(j).start()
        partner_left(j).start()
        across(j, 2).start()
        arrived(j, 3).wait_recv()
        far_across(j).start()
        across(j, 3).start()

    for j in range(NCHUNK - 1):
        for copy in own_copies(j):
            copy.start()
        locals_(j).start()

    def row_copy(k):
        to = peer(*SENDS[k])
        return send(rows_ref.at[to], g_ref.at[r], row_s.at[k], row_r.at[k], to)

    own_rows = pltpu.make_async_copy(rows_ref.at[r], g_ref.at[r], local_s.at[NCHUNK])
    own_rows.start()
    for k in range(len(SENDS)):
        row_copy(k).start()

    total = tile_ref[...]
    for k in range(7):
        tiles[k].wait_recv()
        total = total + tile_in[k]

    @pl.when(c == 0)
    def _():
        panel_in[...] = panel_ref[...]

    @pl.when(c != 0)
    def _():
        panels[0].wait_recv()

    pick = pick_ref[...]
    for part, lo in ((total[:TILE, :], 0), (panel_in[pl.ds(0, TILE), :], 2 * TILE)):
        high = jnp.floor(part * (1.0 / 256.0))
        moved = 256.0 * dot(pick, high.astype(BF16)) + dot(pick, (part - high * 256.0).astype(BF16))
        ext_out[:, :, pl.ds(lo, part.shape[1])] = moved.reshape(16, SLOTS, part.shape[1])
    bx_out[...] = jnp.zeros_like(bx_out)
    bx_out[pl.ds(0, 8), pl.ds(0, TILE)] = total[TILE:, :TILE]
    bx_out[pl.ds(8, 16), :] = panel_in[pl.ds(TILE, 16), :]

    def ext_copy(k):
        to = peer(*SENDS[k])
        return send(ext_out.at[to], ext_ref.at[r], ext_s.at[k], ext_r.at[k], to)

    own_ext = pltpu.make_async_copy(ext_out.at[r], ext_ref.at[r], local_s.at[NCHUNK + 1])
    own_ext.start()
    for copy in own_copies(NCHUNK - 1):
        copy.start()
    locals_(NCHUNK - 1).start()
    for k in range(len(SENDS)):
        ext_copy(k).start()

    for j in range(NCHUNK):
        forward(j)
    for j in range(NCHUNK):
        for k in range(4, 7):
            arrived(j, k).wait_recv()
            across(j, k).start()

    def from_core(j, k):
        there = slices(j, peer(RING[k][0], RING[k][1], 1) if k < 7 else peer(0, 0, 1))[1]
        return send(there, there, ag_s.at[j, 0], core_r.at[j, k], peer(0, 0, 1))

    def row_in(k):
        dx, dh, dc = SENDS[k]
        return g_ref.at[peer(4 - dx, dh, dc)]

    def ext_in(k):
        dx, dh, dc = SENDS[k]
        return ext_ref.at[peer(4 - dx, dh, dc)]

    for j in range(NCHUNK):
        for k in range(8):
            from_core(j, k).wait_recv()
        for copy in own_copies(j):
            copy.wait_send()
        onward_left(j).wait_send()
        partner_right(j).wait_send()
        partner_left(j).wait_send()
        far_across(j).wait_send()
        for k in range(7):
            across(j, k).wait_send()
        locals_(j).wait()
    for k in range(len(SENDS)):
        send(row_in(k), row_in(k), row_s.at[k], row_r.at[k], peer(0, 0, 1)).wait_recv()
        row_copy(k).wait_send()
        send(ext_in(k), ext_in(k), ext_s.at[k], ext_r.at[k], peer(0, 0, 1)).wait_recv()
        ext_copy(k).wait_send()
    own_rows.wait()
    own_ext.wait()
    for t in tiles:
        t.wait_send()

    @pl.when(c == 0)
    def _():
        for p in panels:
            p.wait_send()


def exchange(rows, piv, strip, tile, panel, pick):
    width = rows.shape[2]
    dma = pltpu.SemaphoreType.DMA
    return pl.pallas_call(
        exchange_kernel,
        in_specs=[ANY, ANY, ANY, VM, VM, VM],
        out_specs=[ANY] * 5,
        out_shape=[
            jax.ShapeDtypeStruct((16, SLOTS, width), F32),
            jax.ShapeDtypeStruct((16, SLOTS, 2 * TILE + PANEL), F32),
            jax.ShapeDtypeStruct((2, TILE, width), F32),
            jax.ShapeDtypeStruct((PANEL, width), F32),
            jax.ShapeDtypeStruct((16, 24, PANEL), F32),
        ],
        scratch_shapes=[
            pltpu.VMEM((16, SLOTS, 2 * TILE + PANEL), F32),
            pltpu.VMEM((24, PANEL), F32),
            pltpu.VMEM((7,) + tile.shape, F32),
            pltpu.VMEM(panel.shape, F32),
            dma((7,)), dma((7,)), dma((7,)), dma(()),
            dma((15,)), dma((15,)), dma((15,)), dma((15,)),
            dma((NCHUNK, 15)), dma((NCHUNK, 7)), dma((NCHUNK, 8)), dma((NCHUNK + 2,)),
        ],
        name="exchange",
        compiler_params=pltpu.CompilerParams(collective_id=0, has_side_effects=True),
    )(rows, piv, strip, tile, panel, pick)


def eliminate_kernel(ext_ref, bx_ref, r_ref, big_ref, g_ref, piv_ref, strip_ref, out_ref, hi_ref, lo_ref):
    @pl.when(pl.program_id(0) == 0)
    def _():
        ext = ext_ref[...]
        bx = bx_ref[...]
        b0k1 = limbs(centred(bx[:, 0:8, :TILE].reshape(TILE, TILE)))
        b0p = limbs(centred(bx[:, 8:16, :].reshape(TILE, PANEL)))
        b1p = limbs(centred(bx[:, 16:24, :].reshape(TILE, PANEL)))
        zero = jnp.zeros((ext.shape[0], 1), F32)
        first = limbs(-subtract_product(zero, limbs(centred(ext[:, :TILE])), limbs(centred(r_ref[0]))))
        second = subtract_product(ext[:, TILE : 2 * TILE], first, b0k1)
        second = limbs(-subtract_product(zero, limbs(second), limbs(centred(r_ref[1]))))
        panel = subtract_product(ext[:, 2 * TILE :], first, b0p)
        panel = subtract_product(panel, second, b1p)
        lower = limbs(-subtract_product(zero, limbs(panel), limbs(centred(big_ref[...]))))
        for ref, i in ((hi_ref, 0), (lo_ref, 1)):
            ref[:, pl.ds(0, TILE)] = first[i]
            ref[:, pl.ds(TILE, TILE)] = second[i]
            ref[:, pl.ds(2 * TILE, PANEL)] = lower[i]

    rows = jnp.concatenate([piv_ref[0], piv_ref[1], strip_ref[...]], axis=0)
    result = subtract_product(g_ref[...], (hi_ref[...], lo_ref[...]), limbs(centred(rows)))
    out_ref[...] = jnp.where(result < 0.0, result + MODULUS, result) * INVERSE


def eliminate(ext, bx, recips, big, g, pivs, strips):
    slots, width = g.shape
    block = 512
    inner = 2 * TILE + PANEL
    whole = lambda a: pl.BlockSpec(a.shape, lambda i: (0,) * a.ndim)
    return pl.pallas_call(
        eliminate_kernel,
        grid=(width // block,),
        in_specs=[
            whole(ext), whole(bx), whole(recips), whole(big),
            pl.BlockSpec((slots, block), lambda i: (0, i)),
            pl.BlockSpec((2, TILE, block), lambda i: (0, 0, i)),
            pl.BlockSpec((PANEL, block), lambda i: (0, i)),
        ],
        out_specs=pl.BlockSpec((slots, block), lambda i: (0, i)),
        out_shape=jax.ShapeDtypeStruct((slots, width), F32),
        scratch_shapes=[pltpu.VMEM((slots, inner), BF16)] * 2,
        name="eliminate",
        compiler_params=pltpu.CompilerParams(vmem_limit_bytes=48 << 20),
    )(ext, bx, recips, big, g, pivs, strips)


def local(thin, flags, tiles, pivots, recips, dest, strip, big):
    width = thin.shape[1]
    owned = tiles - lax.axis_index("col") * (width // TILE)
    rows, tile, panel, pick = bucket(owned, flags, thin, dest[None, :], pivots)
    g, ext, pivs, strips, bx = exchange(rows.reshape(16, SLOTS, width), pivots, strip, tile, panel, pick)
    slots = 16 * SLOTS
    return eliminate(
        ext.reshape(slots, -1), bx, recips, big, g.reshape(slots, width), pivs, strips
    )


def solution(mesh):
    return jax.shard_map(
        local,
        mesh=mesh,
        in_specs=(
            P("row", "col"),
            P("row", "col"),
            P(),
            P(None, "row", "col"),
            P(),
            P("row"),
            P("row", "col"),
            P(),
        ),
        out_specs=P("row", "col"),
        check_vma=False,
    )
```

```python
import functools

import jax
import jax.numpy as jnp
from jax import lax
from jax.experimental import pallas as pl
from jax.experimental.pallas import tpu as pltpu
from jax.sharding import PartitionSpec as P

TILE = 128
PANEL = 512
SLOTS = 16
MODULUS = 65521.0
INVERSE = 1.0 / 65521.0
MESH = pl.DeviceIdType.MESH
F32, BF16 = jnp.float32, jnp.bfloat16
ANY = pl.BlockSpec(memory_space=pl.ANY)
VM = pl.BlockSpec(memory_space=pltpu.VMEM)
SM = pl.BlockSpec(memory_space=pltpu.SMEM)


def dot(a, b):
    return jnp.dot(a, b, preferred_element_type=F32)


def nearest(values):
    return values - jnp.floor(values * INVERSE + 0.5) * MODULUS


def centred(values):
    return jnp.where(values > 32760.0, values - MODULUS, values)


def limbs(values):
    high = jnp.floor(values * (1.0 / 256.0) + 0.5)
    return high.astype(BF16), (values - high * 256.0).astype(BF16)


def subtract_product(base, left, right):
    (a_hi, a_lo), (b_hi, b_lo) = left, right
    cross = nearest(nearest(dot(a_hi, b_lo)) + dot(a_lo, b_hi))
    upper = nearest(256.0 * cross + 15.0 * nearest(dot(a_hi, b_hi)))
    return nearest(base - upper - dot(a_lo, b_lo))


def bucket_kernel(owned, flags, x_ref, dest_ref, piv_ref, out_ref, tile_ref, panel_ref, pick_ref):
    step = pl.program_id(0)
    block = x_ref.shape[1]
    tiles = block // TILE

    @pl.when(step == 0)
    def _():
        wide = jnp.broadcast_to(dest_ref[...], (TILE, TILE)).astype(F32)
        earlier = lax.broadcasted_iota(jnp.int32, (TILE, TILE), 0) < lax.broadcasted_iota(jnp.int32, (TILE, TILE), 1)
        same = jnp.where(earlier & (wide == wide.T), 1.0, 0.0)
        place = dest_ref[...].astype(F32) * SLOTS + jnp.sum(same, axis=0, keepdims=True)
        slot = lax.broadcasted_iota(jnp.int32, pick_ref.shape, 0).astype(F32)
        pick_ref[...] = jnp.where(slot == place, 1.0, 0.0).astype(BF16)
        tile_ref[...] = jnp.zeros_like(tile_ref)
        for t in range(PANEL // TILE):
            s = pl.ds(t * TILE, TILE)
            panel_ref[pl.ds(0, TILE), s] = x_ref[:, s] * flags[0, t].astype(F32)
        for k in range(2):
            panel_ref[pl.ds(TILE + 8 * k, 8), :] = piv_ref[k, :, :PANEL]

    pick = pick_ref[...]
    for t in range(tiles):
        s = pl.ds(t * TILE, TILE)
        x = x_ref[:, s] * flags[0, step * tiles + t].astype(F32)
        high = jnp.floor(x * (1.0 / 256.0))
        out_ref[:, s] = 256.0 * dot(pick, high.astype(BF16)) + dot(pick, (x - high * 256.0).astype(BF16))

    for k in range(2):
        tile = owned[k]

        @pl.when((tile >= step * tiles) & (tile < (step + 1) * tiles))
        def _():
            s = pl.ds(pl.multiple_of((tile - step * tiles) * TILE, TILE), TILE)
            tile_ref[pl.ds(0, TILE), pl.ds(k * TILE, TILE)] = x_ref[:, s] * flags[0, tile].astype(F32)
            if k == 1:
                tile_ref[pl.ds(TILE, 8), pl.ds(0, TILE)] = piv_ref[0, :, s]


def bucket(owned, flags, x, dest, piv):
    rows, width = x.shape
    block = 1024
    slots = 16 * SLOTS
    return pl.pallas_call(
        bucket_kernel,
        grid=(width // block,),
        in_specs=[
            SM,
            SM,
            pl.BlockSpec((rows, block), lambda i: (0, i)),
            pl.BlockSpec((1, rows), lambda i: (0, 0)),
            pl.BlockSpec((2, 8, block), lambda i: (0, 0, i)),
        ],
        out_specs=[
            pl.BlockSpec((slots, block), lambda i: (0, i)),
            pl.BlockSpec((rows + 8, 2 * TILE), lambda i: (0, 0)),
            pl.BlockSpec((rows + 16, PANEL), lambda i: (0, 0)),
            pl.BlockSpec((slots, rows), lambda i: (0, 0)),
        ],
        out_shape=[
            jax.ShapeDtypeStruct((slots, width), F32),
            jax.ShapeDtypeStruct((rows + 8, 2 * TILE), F32),
            jax.ShapeDtypeStruct((rows + 16, PANEL), F32),
            jax.ShapeDtypeStruct((slots, rows), BF16),
        ],
        name="bucket",
    )(owned, flags, x, dest, piv)


OTHERS = [(1, 1, 0), (3, 0, 0), (3, 1, 0), (1, 0, 0), (2, 1, 0), (2, 0, 0), (0, 1, 0),
          (1, 1, 1), (3, 0, 1), (3, 1, 1), (1, 0, 1), (2, 1, 1), (2, 0, 1), (0, 1, 1), (0, 0, 1)]
SOURCES = [(3, 0), (1, 0), (0, 1), (2, 0), (3, 1), (1, 1), (2, 1)]
LEFT, RIGHT, PARTNER, FAR = 0, 1, 2, 3
GROUPS = 4
LINES = 48
BLOCK = 512
BX = GROUPS
EXT = 2 * TILE + PANEL


def exchange_kernel(
    rows_ref, piv_ref, strip_ref, tile_ref, panel_ref, pick_ref, r_ref, big_ref,
    out_ref,
    g, lines, ext, bx, ext_out, bx_out, tile_in, panel_in, hi_ref, lo_ref,
    tile_s, tile_r, panel_s, panel_r, row_s, row_r, ext_s, ext_r, ag_s, ag_r, core_r, local_s, out_s,
):
    r, c = lax.axis_index("row"), lax.axis_index("col")
    x, h, core = r // 4, lax.rem(r // 2, 2), lax.rem(r, 2)
    width = rows_ref.shape[2]
    span = width // GROUPS

    def peer(dx, dh, dc):
        return lax.rem(x + dx, 4) * 4 + lax.rem(h + dh, 2) * 2 + lax.rem(core + dc, 2)

    other = peer(0, 0, 1)

    def send(src, dst, ssem, rsem, row, col=c):
        return pltpu.make_async_remote_copy(
            src_ref=src, dst_ref=dst, send_sem=ssem, recv_sem=rsem, device_id=(row, col), device_id_type=MESH
        )

    def took(ref, sem):
        return pltpu.make_async_copy(ref, ref, sem).wait()

    barrier = pltpu.get_barrier_semaphore()
    for off in OTHERS:
        pl.semaphore_signal(barrier, inc=1, device_id=(peer(*off), c), device_id_type=MESH)
    for k in range(1, 8):
        pl.semaphore_signal(barrier, inc=1, device_id=(r, lax.rem(c + k, 8)), device_id_type=MESH)
    pl.semaphore_wait(barrier, len(OTHERS) + 7)

    tiles = [
        send(tile_ref, tile_in.at[k - 1], tile_s.at[k - 1], tile_r.at[k - 1], r, lax.rem(c + k, 8))
        for k in range(1, 8)
    ]
    panels = [send(panel_ref, panel_in, panel_s.at[k - 1], panel_r, r, k) for k in range(1, 8)]
    for t in tiles:
        t.start()

    @pl.when(c == 0)
    def _():
        for p in panels:
            p.start()

    def columns(j):
        return pl.ds(j * span, span)

    def slab(j, row):
        return bx.at[row] if j == BX else lines.at[row, :, columns(j)]

    def pieces(j):
        if j == BX:
            return [(bx_out, bx.at[r])]
        return [
            (piv_ref.at[:, columns(j)], lines.at[r, pl.ds(0, 16), columns(j)]),
            (strip_ref.at[:, columns(j)], lines.at[r, pl.ds(16, LINES - 16), columns(j)]),
        ]

    def own(j):
        for src, dst in pieces(j):
            send(src, dst, ag_s.at[j], ag_r.at[j, LEFT], peer(1, 0, 0)).start()
            send(src, dst, ag_s.at[j], ag_r.at[j, RIGHT], peer(3, 0, 0)).start()
            send(src, dst, ag_s.at[j], ag_r.at[j, PARTNER], peer(0, 1, 0)).start()
            send(src, dst, ag_s.at[j], core_r.at[j], other).start()
            pltpu.make_async_copy(src, dst, local_s.at[j]).start()

    def source(k):
        return peer(SOURCES[k][0], SOURCES[k][1], 0)

    def onward(j, k, rsem, row):
        held = slab(j, source(k))
        send(held, held, ag_s.at[j], rsem, row).start()

    def arrived(j, k):
        took(slab(j, source(k)), ag_r.at[j, k])

    def across(j, k):
        onward(j, k, core_r.at[j], other)

    def forward_near(j):
        odd = lax.rem(x + j, 2) == 1
        arrived(j, LEFT)
        pl.when(odd)(lambda: onward(j, LEFT, ag_r.at[j, FAR], peer(1, 0, 0)))
        across(j, LEFT)
        arrived(j, RIGHT)
        pl.when(jnp.logical_not(odd))(lambda: onward(j, RIGHT, ag_r.at[j, FAR], peer(3, 0, 0)))
        across(j, RIGHT)
        arrived(j, PARTNER)
        onward(j, PARTNER, ag_r.at[j, 4], peer(1, 0, 0))
        onward(j, PARTNER, ag_r.at[j, 5], peer(3, 0, 0))
        across(j, PARTNER)

    def forward_far(j):
        arrived(j, FAR)
        onward(j, FAR, ag_r.at[j, 6], peer(0, 1, 0))
        across(j, FAR)

    def forward_last(j):
        for k in (4, 5, 6):
            arrived(j, k)
            across(j, k)

    def rows_out(j):
        s = columns(j)
        for off in OTHERS:
            to = peer(*off)
            send(rows_ref.at[to, :, s], g.at[r, :, s], row_s.at[j], row_r.at[j], to).start()
        pltpu.make_async_copy(rows_ref.at[r, :, s], g.at[r, :, s], local_s.at[GROUPS + 1 + j]).start()

    def complete(j):
        s = columns(j)
        took(lines.at[pl.ds(0, 8), :, s], core_r.at[j])
        took(slab(j, r), local_s.at[j])
        took(g.at[pl.ds(0, 15), :, s], row_r.at[j])
        took(g.at[0, :, s], local_s.at[GROUPS + 1 + j])

    def compute(j):
        def block(i, _):
            s = pl.ds(pl.multiple_of(j * span + i * BLOCK, BLOCK), BLOCK)
            held = lines[:, :, s]
            rows = jnp.concatenate(
                [held[:, 0:8].reshape(TILE, BLOCK), held[:, 8:16].reshape(TILE, BLOCK),
                 held[:, 16:].reshape(PANEL, BLOCK)], axis=0
            )
            base = g[:, :, s].reshape(16 * SLOTS, BLOCK)
            result = subtract_product(base, (hi_ref[...], lo_ref[...]), limbs(centred(rows)))
            result = jnp.where(result < 0.0, result + MODULUS, result) * INVERSE
            g[:, :, s] = result.reshape(16, SLOTS, BLOCK)
            return 0

        lax.fori_loop(0, span // BLOCK, block, 0)
        pltpu.make_async_copy(g.at[:, :, columns(j)], out_ref.at[:, :, columns(j)], out_s.at[j]).start()

    def panel_columns():
        total = tile_ref[...]
        for k in range(7):
            tiles[k].wait_recv()
            total = total + tile_in[k]

        @pl.when(c == 0)
        def _():
            panel_in[...] = panel_ref[...]

        @pl.when(c != 0)
        def _():
            panels[0].wait_recv()

        pick = pick_ref[...]
        for part, at in ((total[:TILE, :], 0), (panel_in[pl.ds(0, TILE), :], 2 * TILE)):
            high = jnp.floor(part * (1.0 / 256.0))
            moved = 256.0 * dot(pick, high.astype(BF16)) + dot(pick, (part - high * 256.0).astype(BF16))
            ext_out[:, :, pl.ds(at, part.shape[1])] = moved.reshape(16, SLOTS, part.shape[1])
        bx_out[...] = jnp.zeros_like(bx_out)
        bx_out[pl.ds(0, 8), pl.ds(0, TILE)] = total[TILE:, :TILE]
        bx_out[pl.ds(8, 16), :] = panel_in[pl.ds(TILE, 16), :]
        own(BX)
        for off in OTHERS:
            to = peer(*off)
            send(ext_out.at[to], ext.at[r], ext_s, ext_r, to).start()
        pltpu.make_async_copy(ext_out.at[r], ext.at[r], local_s.at[2 * GROUPS + 1]).start()

    def multipliers():
        took(ext.at[pl.ds(0, 15)], ext_r)
        pltpu.make_async_copy(ext_out.at[r], ext.at[r], local_s.at[2 * GROUPS + 1]).wait()
        took(bx.at[pl.ds(0, 8)], core_r.at[BX])
        took(slab(BX, r), local_s.at[BX])
        terms = ext[...].reshape(16 * SLOTS, EXT)
        heads = bx[...]
        b0k1 = limbs(centred(heads[:, 0:8, :TILE].reshape(TILE, TILE)))
        b0p = limbs(centred(heads[:, 8:16, :].reshape(TILE, PANEL)))
        b1p = limbs(centred(heads[:, 16:24, :].reshape(TILE, PANEL)))
        zero = jnp.zeros((16 * SLOTS, 1), F32)
        first = limbs(-subtract_product(zero, limbs(centred(terms[:, :TILE])), limbs(centred(r_ref[0]))))
        second = subtract_product(terms[:, TILE : 2 * TILE], first, b0k1)
        second = limbs(-subtract_product(zero, limbs(second), limbs(centred(r_ref[1]))))
        panel = subtract_product(terms[:, 2 * TILE :], first, b0p)
        panel = subtract_product(panel, second, b1p)
        lower = limbs(-subtract_product(zero, limbs(panel), limbs(centred(big_ref[...]))))
        for ref, i in ((hi_ref, 0), (lo_ref, 1)):
            ref[:, pl.ds(0, TILE)] = first[i]
            ref[:, pl.ds(TILE, TILE)] = second[i]
            ref[:, pl.ds(2 * TILE, PANEL)] = lower[i]

    def begin(j):
        own(j)
        rows_out(j)

    begin(0)
    panel_columns()
    begin(1)
    forward_near(0)
    forward_near(BX)
    begin(2)
    forward_far(0)
    forward_near(1)
    forward_far(BX)
    begin(3)
    forward_last(0)
    forward_far(1)
    forward_near(2)
    forward_last(BX)
    forward_last(1)
    forward_far(2)
    forward_near(3)
    multipliers()
    forward_last(2)
    forward_far(3)
    complete(0)
    compute(0)
    forward_last(3)
    for j in range(1, GROUPS):
        complete(j)
        compute(j)

    for j in range(GROUPS + 1):
        whole = (bx if j == BX else lines.at[:, :, columns(j)])
        took(whole.at[pl.ds(0, 15)], ag_s.at[j])
    for j in range(GROUPS):
        took(g.at[pl.ds(0, 15), :, columns(j)], row_s.at[j])
        pltpu.make_async_copy(g.at[:, :, columns(j)], out_ref.at[:, :, columns(j)], out_s.at[j]).wait()
    took(ext.at[pl.ds(0, 15)], ext_s)
    for t in tiles:
        t.wait_send()

    @pl.when(c == 0)
    def _():
        for p in panels:
            p.wait_send()


def exchange(rows, piv, strip, tile, panel, pick, recips, big):
    width = rows.shape[2]
    dma = pltpu.SemaphoreType.DMA
    return pl.pallas_call(
        exchange_kernel,
        in_specs=[ANY, ANY, ANY, VM, VM, VM, VM, VM],
        out_specs=ANY,
        out_shape=jax.ShapeDtypeStruct((16, SLOTS, width), F32),
        scratch_shapes=[
            pltpu.VMEM((16, SLOTS, width), F32),
            pltpu.VMEM((16, LINES, width), F32),
            pltpu.VMEM((16, SLOTS, EXT), F32),
            pltpu.VMEM((16, 24, PANEL), F32),
            pltpu.VMEM((16, SLOTS, EXT), F32),
            pltpu.VMEM((24, PANEL), F32),
            pltpu.VMEM((7,) + tile.shape, F32),
            pltpu.VMEM(panel.shape, F32),
            pltpu.VMEM((16 * SLOTS, EXT), BF16),
            pltpu.VMEM((16 * SLOTS, EXT), BF16),
            dma((7,)), dma((7,)), dma((7,)), dma(()),
            dma((GROUPS,)), dma((GROUPS,)), dma(()), dma(()),
            dma((GROUPS + 1,)), dma((GROUPS + 1, 7)), dma((GROUPS + 1,)), dma((2 * GROUPS + 2,)), dma((GROUPS,)),
        ],
        name="exchange",
        compiler_params=pltpu.CompilerParams(
            collective_id=0, has_side_effects=True, vmem_limit_bytes=58 << 20
        ),
    )(rows, piv, strip, tile, panel, pick, recips, big)


def local(thin, flags, tiles, pivots, recips, dest, strip, big):
    width = thin.shape[1]
    owned = tiles - lax.axis_index("col") * (width // TILE)
    rows, tile, panel, pick = bucket(owned, flags, thin, dest[None, :], pivots)
    out = exchange(
        rows.reshape(16, SLOTS, width), pivots.reshape(16, width), strip, tile, panel, pick, recips, big
    )
    return out.reshape(16 * SLOTS, width)


def solution(mesh):
    return jax.shard_map(
        local,
        mesh=mesh,
        in_specs=(
            P("row", "col"),
            P("row", "col"),
            P(),
            P(None, "row", "col"),
            P(),
            P("row"),
            P("row", "col"),
            P(),
        ),
        out_specs=P("row", "col"),
        check_vma=False,
    )
```

```python
import functools

import jax
import jax.numpy as jnp
from jax import lax
from jax.experimental import pallas as pl
from jax.experimental.pallas import tpu as pltpu
from jax.sharding import PartitionSpec as P

TILE = 128
PANEL = 512
SLOTS = 16
MODULUS = 65521.0
INVERSE = 1.0 / 65521.0
MESH = pl.DeviceIdType.MESH
F32, BF16 = jnp.float32, jnp.bfloat16
ANY = pl.BlockSpec(memory_space=pl.ANY)
VM = pl.BlockSpec(memory_space=pltpu.VMEM)
SM = pl.BlockSpec(memory_space=pltpu.SMEM)


def dot(a, b):
    return jnp.dot(a, b, preferred_element_type=F32)


def nearest(values):
    return values - jnp.floor(values * INVERSE + 0.5) * MODULUS


def centred(values):
    return jnp.where(values > 32760.0, values - MODULUS, values)


def limbs(values):
    high = jnp.floor(values * (1.0 / 256.0) + 0.5)
    return high.astype(BF16), (values - high * 256.0).astype(BF16)


def subtract_product(base, left, right):
    (a_hi, a_lo), (b_hi, b_lo) = left, right
    cross = nearest(nearest(dot(a_hi, b_lo)) + dot(a_lo, b_hi))
    upper = nearest(256.0 * cross + 15.0 * nearest(dot(a_hi, b_hi)))
    return nearest(base - upper - dot(a_lo, b_lo))


OTHERS = [(1, 1, 0), (3, 0, 0), (3, 1, 0), (1, 0, 0), (2, 1, 0), (2, 0, 0), (0, 1, 0),
          (1, 1, 1), (3, 0, 1), (3, 1, 1), (1, 0, 1), (2, 1, 1), (2, 0, 1), (0, 1, 1), (0, 0, 1)]
SOURCES = [(3, 0), (1, 0), (0, 1), (2, 0), (3, 1), (1, 1), (2, 1)]
LEFT, RIGHT, PARTNER, FAR = 0, 1, 2, 3
SPANS = [2048, 2048, 2048, 1024, 1024]
GROUPS = len(SPANS)
LINES = 48
BLOCK = 512
HEAD = SLOTS + 8


def exchange_kernel(
    owned, flags, dest_ref, thin_ref, piv_ref, strip_ref, r_hbm, big_hbm,
    g,
    lines, rows, thin, ext, ext_out, tile, tile_sum, tile_in, low, hi_ref, lo_ref, pick_ref, r_ref, big_ref,
    tile_s, tile_r, low_s, low_r, row_s, row_r, ext_s, ext_r, ag_s, ag_r, core_r, ag_l, row_l, ext_l, in_l, big_l,
):
    r, c = lax.axis_index("row"), lax.axis_index("col")
    x, h, core = r // 4, lax.rem(r // 2, 2), lax.rem(r, 2)
    plane, y = c // 4, lax.rem(c, 4)

    def columns(j):
        return pl.ds(sum(SPANS[:j]), SPANS[j])

    def thin_in(j):
        return pltpu.make_async_copy(thin_ref.at[:, columns(j)], thin.at[:, columns(j)], in_l.at[j])

    constants = [
        pltpu.make_async_copy(r_hbm, r_ref, big_l.at[0]),
        pltpu.make_async_copy(big_hbm, big_ref, big_l.at[1]),
    ]
    for j in range(GROUPS):
        thin_in(j).start()
    for copy in constants:
        copy.start()

    def peer(dx, dh, dc):
        return lax.rem(x + dx, 4) * 4 + lax.rem(h + dh, 2) * 2 + lax.rem(core + dc, 2)

    other = peer(0, 0, 1)
    across_z = lax.rem(c + 4, 8)

    def along_y(k):
        return plane * 4 + lax.rem(y + k, 4)

    def send(src, dst, ssem, rsem, row, col=c):
        return pltpu.make_async_remote_copy(
            src_ref=src, dst_ref=dst, send_sem=ssem, recv_sem=rsem, device_id=(row, col), device_id_type=MESH
        )

    def took(ref, sem):
        pltpu.make_async_copy(ref, ref, sem).wait()

    barrier = pltpu.get_barrier_semaphore()
    for off in OTHERS:
        pl.semaphore_signal(barrier, inc=1, device_id=(peer(*off), c), device_id_type=MESH)
    for col in (across_z, along_y(1), along_y(2), along_y(3)):
        pl.semaphore_signal(barrier, inc=1, device_id=(r, col), device_id_type=MESH)
    pl.semaphore_wait(barrier, len(OTHERS) + 4)

    def slab(j, row):
        return lines.at[row, :, columns(j)]

    def own(j):
        for src, dst in (
            (piv_ref.at[:, columns(j)], lines.at[r, pl.ds(0, 16), columns(j)]),
            (strip_ref.at[:, columns(j)], lines.at[r, pl.ds(16, LINES - 16), columns(j)]),
        ):
            send(src, dst, ag_s.at[j], ag_r.at[j, PARTNER], peer(0, 1, 0)).start()
            send(src, dst, ag_s.at[j], ag_r.at[j, LEFT], peer(1, 0, 0)).start()
            send(src, dst, ag_s.at[j], ag_r.at[j, RIGHT], peer(3, 0, 0)).start()
            send(src, dst, ag_s.at[j], core_r.at[j], other).start()
            pltpu.make_async_copy(src, dst, ag_l.at[j]).start()

    def source(k):
        return peer(SOURCES[k][0], SOURCES[k][1], 0)

    def onward(j, k, rsem, row):
        held = slab(j, source(k))
        send(held, held, ag_s.at[j], rsem, row).start()

    def arrived(j, k):
        took(slab(j, source(k)), ag_r.at[j, k])

    def across(j, k):
        onward(j, k, core_r.at[j], other)

    def near(j):
        odd = lax.rem(x + j, 2) == 1
        arrived(j, LEFT)
        pl.when(odd)(lambda: onward(j, LEFT, ag_r.at[j, FAR], peer(1, 0, 0)))
        across(j, LEFT)
        arrived(j, RIGHT)
        pl.when(jnp.logical_not(odd))(lambda: onward(j, RIGHT, ag_r.at[j, FAR], peer(3, 0, 0)))
        across(j, RIGHT)
        arrived(j, PARTNER)
        onward(j, PARTNER, ag_r.at[j, 4], peer(1, 0, 0))
        onward(j, PARTNER, ag_r.at[j, 5], peer(3, 0, 0))
        across(j, PARTNER)

    def far(j):
        arrived(j, FAR)
        onward(j, FAR, ag_r.at[j, 6], peer(0, 1, 0))
        across(j, FAR)

    def last(j):
        for k in (4, 5, 6):
            arrived(j, k)
            across(j, k)

    def choose():
        wide = jnp.broadcast_to(dest_ref[...], (TILE, TILE)).astype(F32)
        earlier = lax.broadcasted_iota(jnp.int32, (TILE, TILE), 0) < lax.broadcasted_iota(jnp.int32, (TILE, TILE), 1)
        same = jnp.where(earlier & (wide == wide.T), 1.0, 0.0)
        place = dest_ref[...].astype(F32) * SLOTS + jnp.sum(same, axis=0, keepdims=True)
        slot = lax.broadcasted_iota(jnp.int32, pick_ref.shape, 0).astype(F32)
        pick_ref[...] = jnp.where(slot == place, 1.0, 0.0).astype(BF16)

    def picked(part):
        high = jnp.floor(part * (1.0 / 256.0))
        moved = 256.0 * dot(pick_ref[...], high.astype(BF16)) + dot(pick_ref[...], (part - high * 256.0).astype(BF16))
        return moved.reshape(16, SLOTS, part.shape[1])

    def flag(t):
        return flags[0, t].astype(F32)

    def fill(j):
        start = sum(SPANS[:j])

        def block(i, _):
            s = pl.ds(pl.multiple_of(start + i * BLOCK, BLOCK), BLOCK)
            first = start // TILE + i * (BLOCK // TILE)
            mask = jnp.concatenate([jnp.full((1, TILE), flag(first + t), F32) for t in range(BLOCK // TILE)], axis=1)
            part = thin[:, s] * mask
            rows[:, :, s] = picked(part)
            for t in range(BLOCK // TILE):
                for k in range(2):
                    chosen = jnp.where(owned[k] == first + t, 1.0, 0.0)
                    into = pl.ds(0, TILE), pl.ds(k * TILE, TILE)
                    tile[into] += part[:, t * TILE : (t + 1) * TILE] * chosen
                at = pl.multiple_of(start + i * BLOCK + t * TILE, TILE)
                tile[pl.ds(TILE, 8), pl.ds(0, TILE)] += piv_ref[pl.ds(0, 8), pl.ds(at, TILE)] * chosen
            return 0

        lax.fori_loop(0, SPANS[j] // BLOCK, block, 0)

    def rows_out(j):
        s = columns(j)
        for off in OTHERS:
            to = peer(*off)
            send(rows.at[to, :, s], g.at[r, :, s], row_s.at[j], row_r.at[j], to).start()
        pltpu.make_async_copy(rows.at[r, :, s], g.at[r, :, s], row_l.at[j]).start()

    def tile_across():
        return send(tile, tile_in.at[0], tile_s.at[0], tile_r.at[0], r, across_z)

    def tile_along(k):
        return send(tile_sum, tile_in.at[k], tile_s.at[k], tile_r.at[k], r, along_y(k))

    def tile_next():
        tile_across().wait_recv()
        tile_sum[...] = tile[...] + tile_in[0]
        for k in (1, 2, 3):
            tile_along(k).start()

    def ext_begin():
        total = tile_sum[...]
        for k in (1, 2, 3):
            tile_along(k).wait_recv()
            total = total + tile_in[k]
        ext_out[:, pl.ds(0, SLOTS), :] = picked(total[:TILE, :])
        ext_out[:, pl.ds(SLOTS, 8), :] = jnp.broadcast_to(total[TILE:, :][None], (16, 8, 2 * TILE))
        for off in OTHERS:
            to = peer(*off)
            send(ext_out.at[to], ext.at[r], ext_s, ext_r, to).start()
        pltpu.make_async_copy(ext_out.at[r], ext.at[r], ext_l).start()

    def keep(parts, at):
        for ref, part in zip((hi_ref, lo_ref), parts):
            ref[:, pl.ds(at, part.shape[1])] = part

    def kept(at):
        return hi_ref[:, pl.ds(at, TILE)], lo_ref[:, pl.ds(at, TILE)]

    zero = jnp.zeros((16 * SLOTS, 1), F32)

    def factors():
        took(ext.at[pl.ds(0, 15)], ext_r)
        took(ext.at[0], ext_l)
        for copy in constants:
            copy.wait()
        terms = ext[:, :SLOTS, :].reshape(16 * SLOTS, 2 * TILE)
        pivot = limbs(centred(ext[:, SLOTS:, :TILE].reshape(TILE, TILE)))
        first = limbs(-subtract_product(zero, limbs(centred(terms[:, :TILE])), limbs(centred(r_ref[0]))))
        second = subtract_product(terms[:, TILE:], first, pivot)
        second = limbs(-subtract_product(zero, limbs(second), limbs(centred(r_ref[1]))))
        keep(first, 0)
        keep(second, TILE)

    def low_out(k):
        col = (1, 2, 3, 4)[k]
        return send(low, low, low_s.at[k], low_r, r, col)

    def low_next(k):
        return send(low, low, low_s.at[k], low_r, r, 5 + k)

    def lower_begin():
        @pl.when(c == 0)
        def _():
            base = g[:, :, :PANEL].reshape(16 * SLOTS, PANEL)
            for k in range(2):
                part = lines[:, 8 * k : 8 * k + 8, :PANEL].reshape(TILE, PANEL)
                base = subtract_product(base, kept(k * TILE), limbs(centred(part)))
            low[...] = -subtract_product(zero, limbs(base), limbs(centred(big_ref[...])))
            for k in (3, 0, 1, 2):
                low_out(k).start()

        @pl.when(c == 4)
        def _():
            low_out(3).wait_recv()
            for k in range(3):
                low_next(k).start()

    def lower_end():
        @pl.when((c != 0) & (c != 4))
        def _():
            low_out(3).wait_recv()

        keep(limbs(low[...]), 2 * TILE)

    def complete(j):
        s = columns(j)
        took(lines.at[pl.ds(0, 8), :, s], core_r.at[j])
        took(slab(j, r), ag_l.at[j])
        took(g.at[pl.ds(0, 15), :, s], row_r.at[j])
        took(g.at[0, :, s], row_l.at[j])

    def compute(j):
        start = sum(SPANS[:j])

        def block(i, _):
            s = pl.ds(pl.multiple_of(start + i * BLOCK, BLOCK), BLOCK)
            held = lines[:, :, s]
            inner = jnp.concatenate(
                [held[:, 0:8].reshape(TILE, BLOCK), held[:, 8:16].reshape(TILE, BLOCK),
                 held[:, 16:].reshape(PANEL, BLOCK)], axis=0
            )
            base = g[:, :, s].reshape(16 * SLOTS, BLOCK)
            result = subtract_product(base, (hi_ref[...], lo_ref[...]), limbs(centred(inner)))
            result = jnp.where(result < 0.0, result + MODULUS, result) * INVERSE
            g[:, :, s] = result.reshape(16, SLOTS, BLOCK)
            return 0

        lax.fori_loop(0, SPANS[j] // BLOCK, block, 0)

    for j in range(GROUPS):
        own(j)
    choose()
    tile[...] = jnp.zeros_like(tile)
    for j in range(GROUPS):
        thin_in(j).wait()
    fill(0)
    rows_out(0)
    for j in range(1, GROUPS):
        fill(j)
    tile_across().start()
    near(0)
    near(1)
    rows_out(1)
    tile_next()
    near(2)
    far(0)
    ext_begin()
    near(3)
    far(1)
    near(4)
    rows_out(2)
    far(2)
    last(0)
    far(3)
    last(1)
    rows_out(3)
    factors()
    far(4)
    last(2)
    rows_out(4)
    complete(0)
    lower_begin()
    last(3)
    last(4)
    lower_end()
    compute(0)
    for j in range(1, GROUPS):
        complete(j)
        compute(j)

    for j in range(GROUPS):
        took(lines.at[pl.ds(0, 15), :, columns(j)], ag_s.at[j])
        took(g.at[pl.ds(0, 15), :, columns(j)], row_s.at[j])
    took(ext.at[pl.ds(0, 15)], ext_s)
    tile_across().wait_send()
    for k in (1, 2, 3):
        tile_along(k).wait_send()

    @pl.when(c == 0)
    def _():
        for k in range(4):
            low_out(k).wait_send()

    @pl.when(c == 4)
    def _():
        for k in range(3):
            low_next(k).wait_send()


def exchange(owned, flags, dest, thin, piv, strip, recips, big):
    width = thin.shape[1]
    dma = pltpu.SemaphoreType.DMA
    head = (TILE + 8, 2 * TILE)
    return pl.pallas_call(
        exchange_kernel,
        in_specs=[SM, SM, VM, ANY, VM, ANY, ANY, ANY],
        out_specs=VM,
        out_shape=pltpu.VMEM((16, SLOTS, width), F32),
        scratch_shapes=[
            pltpu.VMEM((16, LINES, width), F32),
            pltpu.VMEM((16, SLOTS, width), F32),
            pltpu.VMEM(thin.shape, F32),
            pltpu.VMEM((16, HEAD, 2 * TILE), F32),
            pltpu.VMEM((16, HEAD, 2 * TILE), F32),
            pltpu.VMEM(head, F32),
            pltpu.VMEM(head, F32),
            pltpu.VMEM((4,) + head, F32),
            pltpu.VMEM((16 * SLOTS, PANEL), F32),
            pltpu.VMEM((16 * SLOTS, 2 * TILE + PANEL), BF16),
            pltpu.VMEM((16 * SLOTS, 2 * TILE + PANEL), BF16),
            pltpu.VMEM((16 * SLOTS, TILE), BF16),
            pltpu.VMEM(recips.shape, F32),
            pltpu.VMEM(big.shape, F32),
            dma((4,)), dma((4,)), dma((4,)), dma(()),
            dma((GROUPS,)), dma((GROUPS,)), dma(()), dma(()),
            dma((GROUPS,)), dma((GROUPS, 7)), dma((GROUPS,)),
            dma((GROUPS,)), dma((GROUPS,)), dma(()), dma((GROUPS,)), dma((2,)),
        ],
        name="exchange",
        compiler_params=pltpu.CompilerParams(
            collective_id=0, has_side_effects=True, vmem_limit_bytes=52 << 20
        ),
    )(owned, flags, dest, thin, piv, strip, recips, big)


def local(thin, flags, tiles, pivots, recips, dest, strip, big):
    width = thin.shape[1]
    owned = tiles - lax.axis_index("col") * (width // TILE)
    out = exchange(owned, flags, dest[None, :], thin, pivots.reshape(16, width), strip, recips, big)
    return out.reshape(16 * SLOTS, width)


def solution(mesh):
    return jax.shard_map(
        local,
        mesh=mesh,
        in_specs=(
            P("row", "col"),
            P("row", "col"),
            P(),
            P(None, "row", "col"),
            P(),
            P("row"),
            P("row", "col"),
            P(),
        ),
        out_specs=P("row", "col"),
        check_vma=False,
    )
```

```python
import functools

import jax
import jax.numpy as jnp
from jax import lax
from jax.experimental import pallas as pl
from jax.experimental.pallas import tpu as pltpu
from jax.sharding import PartitionSpec as P

TILE = 128
PANEL = 512
SLOTS = 16
MODULUS = 65521.0
INVERSE = 1.0 / 65521.0
MESH = pl.DeviceIdType.MESH
F32, BF16 = jnp.float32, jnp.bfloat16
ANY = pl.BlockSpec(memory_space=pl.ANY)
VM = pl.BlockSpec(memory_space=pltpu.VMEM)
SM = pl.BlockSpec(memory_space=pltpu.SMEM)


def dot(a, b):
    return jnp.dot(a, b, preferred_element_type=F32)


def nearest(values):
    return values - jnp.floor(values * INVERSE + 0.5) * MODULUS


def centred(values):
    return jnp.where(values > 32760.0, values - MODULUS, values)


def limbs(values):
    high = jnp.floor(values * (1.0 / 256.0) + 0.5)
    return high.astype(BF16), (values - high * 256.0).astype(BF16)


def subtract_product(base, left, right):
    (a_hi, a_lo), (b_hi, b_lo) = left, right
    cross = nearest(nearest(dot(a_hi, b_lo)) + dot(a_lo, b_hi))
    upper = nearest(256.0 * cross + 15.0 * nearest(dot(a_hi, b_hi)))
    return nearest(base - upper - dot(a_lo, b_lo))


OTHERS = [(1, 1, 0), (3, 0, 0), (3, 1, 0), (1, 0, 0), (2, 1, 0), (2, 0, 0), (0, 1, 0),
          (1, 1, 1), (3, 0, 1), (3, 1, 1), (1, 0, 1), (2, 1, 1), (2, 0, 1), (0, 1, 1), (0, 0, 1)]
SOURCES = [(3, 0), (1, 0), (0, 1), (2, 0), (3, 1), (1, 1), (2, 1)]
LEFT, RIGHT, PARTNER, FAR = 0, 1, 2, 3
SPANS = [512, 2560, 2048, 1536, 1024, 512]
GROUPS = len(SPANS)
LINES = 48
BLOCK = 512
HEAD = SLOTS + 8


def exchange_kernel(
    owned, flags, dest_ref, thin_ref, piv_ref, strip_ref, r_hbm, big_hbm,
    g,
    lines, rows, thin, ext, ext_out, tile, tile_sum, tile_in, low, hi_ref, lo_ref, pick_ref, r_ref, big_ref,
    tile_s, tile_r, low_s, low_r, row_s, row_r, ext_s, ext_r, ag_s, ag_r, core_r, ag_l, row_l, ext_l, in_l, big_l,
):
    r, c = lax.axis_index("row"), lax.axis_index("col")
    x, h, core = r // 4, lax.rem(r // 2, 2), lax.rem(r, 2)
    plane, y = c // 4, lax.rem(c, 4)

    def columns(j):
        return pl.ds(sum(SPANS[:j]), SPANS[j])

    def thin_in(j):
        return pltpu.make_async_copy(thin_ref.at[:, columns(j)], thin.at[:, columns(j)], in_l.at[j])

    constants = [
        pltpu.make_async_copy(r_hbm, r_ref, big_l.at[0]),
        pltpu.make_async_copy(big_hbm, big_ref, big_l.at[1]),
    ]
    for j in range(GROUPS):
        thin_in(j).start()
    for copy in constants:
        copy.start()

    def peer(dx, dh, dc):
        return lax.rem(x + dx, 4) * 4 + lax.rem(h + dh, 2) * 2 + lax.rem(core + dc, 2)

    other = peer(0, 0, 1)
    across_z = lax.rem(c + 4, 8)

    def along_y(k):
        return plane * 4 + lax.rem(y + k, 4)

    def send(src, dst, ssem, rsem, row, col=c):
        return pltpu.make_async_remote_copy(
            src_ref=src, dst_ref=dst, send_sem=ssem, recv_sem=rsem, device_id=(row, col), device_id_type=MESH
        )

    def took(ref, sem):
        pltpu.make_async_copy(ref, ref, sem).wait()

    barrier = pltpu.get_barrier_semaphore()
    for off in OTHERS:
        pl.semaphore_signal(barrier, inc=1, device_id=(peer(*off), c), device_id_type=MESH)
    for col in (across_z, along_y(1), along_y(2), along_y(3)):
        pl.semaphore_signal(barrier, inc=1, device_id=(r, col), device_id_type=MESH)
    pl.semaphore_wait(barrier, len(OTHERS) + 4)

    def slab(j, row):
        return lines.at[row, :, columns(j)]

    def own(j):
        for src, dst in (
            (piv_ref.at[:, columns(j)], lines.at[r, pl.ds(0, 16), columns(j)]),
            (strip_ref.at[:, columns(j)], lines.at[r, pl.ds(16, LINES - 16), columns(j)]),
        ):
            send(src, dst, ag_s.at[j], ag_r.at[j, PARTNER], peer(0, 1, 0)).start()
            send(src, dst, ag_s.at[j], ag_r.at[j, LEFT], peer(1, 0, 0)).start()
            send(src, dst, ag_s.at[j], ag_r.at[j, RIGHT], peer(3, 0, 0)).start()
            send(src, dst, ag_s.at[j], core_r.at[j], other).start()
            pltpu.make_async_copy(src, dst, ag_l.at[j]).start()

    def source(k):
        return peer(SOURCES[k][0], SOURCES[k][1], 0)

    def onward(j, k, rsem, row):
        held = slab(j, source(k))
        send(held, held, ag_s.at[j], rsem, row).start()

    def arrived(j, k):
        took(slab(j, source(k)), ag_r.at[j, k])

    def across(j, k):
        onward(j, k, core_r.at[j], other)

    def near(j):
        odd = lax.rem(x + j, 2) == 1
        arrived(j, LEFT)
        pl.when(odd)(lambda: onward(j, LEFT, ag_r.at[j, FAR], peer(1, 0, 0)))
        across(j, LEFT)
        arrived(j, RIGHT)
        pl.when(jnp.logical_not(odd))(lambda: onward(j, RIGHT, ag_r.at[j, FAR], peer(3, 0, 0)))
        across(j, RIGHT)
        arrived(j, PARTNER)
        onward(j, PARTNER, ag_r.at[j, 4], peer(1, 0, 0))
        onward(j, PARTNER, ag_r.at[j, 5], peer(3, 0, 0))
        across(j, PARTNER)

    def far(j):
        arrived(j, FAR)
        onward(j, FAR, ag_r.at[j, 6], peer(0, 1, 0))
        across(j, FAR)

    def last(j):
        for k in (4, 5, 6):
            arrived(j, k)
            across(j, k)

    def choose():
        wide = jnp.broadcast_to(dest_ref[...], (TILE, TILE)).astype(F32)
        earlier = lax.broadcasted_iota(jnp.int32, (TILE, TILE), 0) < lax.broadcasted_iota(jnp.int32, (TILE, TILE), 1)
        same = jnp.where(earlier & (wide == wide.T), 1.0, 0.0)
        place = dest_ref[...].astype(F32) * SLOTS + jnp.sum(same, axis=0, keepdims=True)
        slot = lax.broadcasted_iota(jnp.int32, pick_ref.shape, 0).astype(F32)
        pick_ref[...] = jnp.where(slot == place, 1.0, 0.0).astype(BF16)

    def picked(part):
        high = jnp.floor(part * (1.0 / 256.0))
        moved = 256.0 * dot(pick_ref[...], high.astype(BF16)) + dot(pick_ref[...], (part - high * 256.0).astype(BF16))
        return moved.reshape(16, SLOTS, part.shape[1])

    def flag(t):
        return flags[0, t].astype(F32)

    def fill(j):
        start = sum(SPANS[:j])

        def block(i, _):
            s = pl.ds(pl.multiple_of(start + i * BLOCK, BLOCK), BLOCK)
            first = start // TILE + i * (BLOCK // TILE)
            mask = jnp.concatenate([jnp.full((1, TILE), flag(first + t), F32) for t in range(BLOCK // TILE)], axis=1)
            part = thin[:, s] * mask
            rows[:, :, s] = picked(part)
            for t in range(BLOCK // TILE):
                for k in range(2):
                    chosen = jnp.where(owned[k] == first + t, 1.0, 0.0)
                    into = pl.ds(0, TILE), pl.ds(k * TILE, TILE)
                    tile[into] += part[:, t * TILE : (t + 1) * TILE] * chosen
                at = pl.multiple_of(start + i * BLOCK + t * TILE, TILE)
                tile[pl.ds(TILE, 8), pl.ds(0, TILE)] += piv_ref[pl.ds(0, 8), pl.ds(at, TILE)] * chosen
            return 0

        lax.fori_loop(0, SPANS[j] // BLOCK, block, 0)

    def rows_out(j):
        s = columns(j)
        for off in OTHERS:
            to = peer(*off)
            send(rows.at[to, :, s], g.at[r, :, s], row_s.at[j], row_r.at[j], to).start()
        pltpu.make_async_copy(rows.at[r, :, s], g.at[r, :, s], row_l.at[j]).start()

    def tile_across():
        return send(tile, tile_in.at[0], tile_s.at[0], tile_r.at[0], r, across_z)

    def tile_along(k):
        return send(tile_sum, tile_in.at[k], tile_s.at[k], tile_r.at[k], r, along_y(k))

    def tile_next():
        tile_across().wait_recv()
        tile_sum[...] = tile[...] + tile_in[0]
        for k in (1, 2, 3):
            tile_along(k).start()

    def ext_begin():
        total = tile_sum[...]
        for k in (1, 2, 3):
            tile_along(k).wait_recv()
            total = total + tile_in[k]
        ext_out[:, pl.ds(0, SLOTS), :] = picked(total[:TILE, :])
        ext_out[:, pl.ds(SLOTS, 8), :] = jnp.broadcast_to(total[TILE:, :][None], (16, 8, 2 * TILE))
        for off in OTHERS:
            to = peer(*off)
            send(ext_out.at[to], ext.at[r], ext_s, ext_r, to).start()
        pltpu.make_async_copy(ext_out.at[r], ext.at[r], ext_l).start()

    def keep(parts, at):
        for ref, part in zip((hi_ref, lo_ref), parts):
            ref[:, pl.ds(at, part.shape[1])] = part

    def kept(at):
        return hi_ref[:, pl.ds(at, TILE)], lo_ref[:, pl.ds(at, TILE)]

    zero = jnp.zeros((16 * SLOTS, 1), F32)

    def factors():
        took(ext.at[pl.ds(0, 15)], ext_r)
        took(ext.at[0], ext_l)
        for copy in constants:
            copy.wait()
        terms = ext[:, :SLOTS, :].reshape(16 * SLOTS, 2 * TILE)
        pivot = limbs(centred(ext[:, SLOTS:, :TILE].reshape(TILE, TILE)))
        first = limbs(-subtract_product(zero, limbs(centred(terms[:, :TILE])), limbs(centred(r_ref[0]))))
        second = subtract_product(terms[:, TILE:], first, pivot)
        second = limbs(-subtract_product(zero, limbs(second), limbs(centred(r_ref[1]))))
        keep(first, 0)
        keep(second, TILE)

    def low_out(k):
        col = (1, 2, 3, 4)[k]
        return send(low, low, low_s.at[k], low_r, r, col)

    def low_next(k):
        return send(low, low, low_s.at[k], low_r, r, 5 + k)

    def lower_begin():
        @pl.when(c == 0)
        def _():
            base = g[:, :, :PANEL].reshape(16 * SLOTS, PANEL)
            for k in range(2):
                part = lines[:, 8 * k : 8 * k + 8, :PANEL].reshape(TILE, PANEL)
                base = subtract_product(base, kept(k * TILE), limbs(centred(part)))
            low[...] = -subtract_product(zero, limbs(base), limbs(centred(big_ref[...])))
            for k in (3, 0, 1, 2):
                low_out(k).start()

        @pl.when(c == 4)
        def _():
            low_out(3).wait_recv()
            for k in range(3):
                low_next(k).start()

    def lower_end():
        @pl.when((c != 0) & (c != 4))
        def _():
            low_out(3).wait_recv()

        keep(limbs(low[...]), 2 * TILE)

    def complete(j):
        s = columns(j)
        took(lines.at[pl.ds(0, 8), :, s], core_r.at[j])
        took(slab(j, r), ag_l.at[j])
        took(g.at[pl.ds(0, 15), :, s], row_r.at[j])
        took(g.at[0, :, s], row_l.at[j])

    def compute(j):
        start = sum(SPANS[:j])

        def block(i, _):
            s = pl.ds(pl.multiple_of(start + i * BLOCK, BLOCK), BLOCK)
            held = lines[:, :, s]
            inner = jnp.concatenate(
                [held[:, 0:8].reshape(TILE, BLOCK), held[:, 8:16].reshape(TILE, BLOCK),
                 held[:, 16:].reshape(PANEL, BLOCK)], axis=0
            )
            base = g[:, :, s].reshape(16 * SLOTS, BLOCK)
            result = subtract_product(base, (hi_ref[...], lo_ref[...]), limbs(centred(inner)))
            result = jnp.where(result < 0.0, result + MODULUS, result) * INVERSE
            g[:, :, s] = result.reshape(16, SLOTS, BLOCK)
            return 0

        lax.fori_loop(0, SPANS[j] // BLOCK, block, 0)

    own(0)
    own(1)
    choose()
    tile[...] = jnp.zeros_like(tile)
    for j in range(GROUPS):
        thin_in(j).wait()
    fill(0)
    rows_out(0)
    near(0)
    fill(1)
    fill(2)
    far(0)
    fill(3)
    fill(4)
    fill(5)
    tile_across().start()
    last(0)
    own(2)
    own(3)
    near(1)
    tile_next()
    own(4)
    own(5)
    ext_begin()
    near(2)
    rows_out(1)
    far(1)
    near(3)
    factors()
    complete(0)
    lower_begin()
    near(4)
    near(5)
    far(2)
    rows_out(2)
    last(1)
    far(3)
    last(2)
    rows_out(3)
    far(4)
    far(5)
    rows_out(4)
    rows_out(5)
    lower_end()
    compute(0)
    last(3)
    complete(1)
    compute(1)
    last(4)
    complete(2)
    compute(2)
    last(5)
    complete(3)
    compute(3)
    complete(4)
    compute(4)
    complete(5)
    compute(5)

    for j in range(GROUPS):
        took(lines.at[pl.ds(0, 15), :, columns(j)], ag_s.at[j])
        took(g.at[pl.ds(0, 15), :, columns(j)], row_s.at[j])
    took(ext.at[pl.ds(0, 15)], ext_s)
    tile_across().wait_send()
    for k in (1, 2, 3):
        tile_along(k).wait_send()

    @pl.when(c == 0)
    def _():
        for k in range(4):
            low_out(k).wait_send()

    @pl.when(c == 4)
    def _():
        for k in range(3):
            low_next(k).wait_send()


def exchange(owned, flags, dest, thin, piv, strip, recips, big):
    width = thin.shape[1]
    dma = pltpu.SemaphoreType.DMA
    head = (TILE + 8, 2 * TILE)
    return pl.pallas_call(
        exchange_kernel,
        in_specs=[SM, SM, VM, ANY, VM, ANY, ANY, ANY],
        out_specs=VM,
        out_shape=pltpu.VMEM((16, SLOTS, width), F32),
        scratch_shapes=[
            pltpu.VMEM((16, LINES, width), F32),
            pltpu.VMEM((16, SLOTS, width), F32),
            pltpu.VMEM(thin.shape, F32),
            pltpu.VMEM((16, HEAD, 2 * TILE), F32),
            pltpu.VMEM((16, HEAD, 2 * TILE), F32),
            pltpu.VMEM(head, F32),
            pltpu.VMEM(head, F32),
            pltpu.VMEM((4,) + head, F32),
            pltpu.VMEM((16 * SLOTS, PANEL), F32),
            pltpu.VMEM((16 * SLOTS, 2 * TILE + PANEL), BF16),
            pltpu.VMEM((16 * SLOTS, 2 * TILE + PANEL), BF16),
            pltpu.VMEM((16 * SLOTS, TILE), BF16),
            pltpu.VMEM(recips.shape, F32),
            pltpu.VMEM(big.shape, F32),
            dma((4,)), dma((4,)), dma((4,)), dma(()),
            dma((GROUPS,)), dma((GROUPS,)), dma(()), dma(()),
            dma((GROUPS,)), dma((GROUPS, 7)), dma((GROUPS,)),
            dma((GROUPS,)), dma((GROUPS,)), dma(()), dma((GROUPS,)), dma((2,)),
        ],
        name="exchange",
        compiler_params=pltpu.CompilerParams(
            collective_id=0, has_side_effects=True, vmem_limit_bytes=52 << 20
        ),
    )(owned, flags, dest, thin, piv, strip, recips, big)


def local(thin, flags, tiles, pivots, recips, dest, strip, big):
    width = thin.shape[1]
    owned = tiles - lax.axis_index("col") * (width // TILE)
    out = exchange(owned, flags, dest[None, :], thin, pivots.reshape(16, width), strip, recips, big)
    return out.reshape(16 * SLOTS, width)


def solution(mesh):
    return jax.shard_map(
        local,
        mesh=mesh,
        in_specs=(
            P("row", "col"),
            P("row", "col"),
            P(),
            P(None, "row", "col"),
            P(),
            P("row"),
            P("row", "col"),
            P(),
        ),
        out_specs=P("row", "col"),
        check_vma=False,
    )
```

```python
import functools

import jax
import jax.numpy as jnp
from jax import lax
from jax.experimental import pallas as pl
from jax.experimental.pallas import tpu as pltpu
from jax.sharding import PartitionSpec as P

TILE = 128
PANEL = 512
SLOTS = 16
MODULUS = 65521.0
INVERSE = 1.0 / 65521.0
MESH = pl.DeviceIdType.MESH
F32, BF16 = jnp.float32, jnp.bfloat16
ANY = pl.BlockSpec(memory_space=pl.ANY)
VM = pl.BlockSpec(memory_space=pltpu.VMEM)
SM = pl.BlockSpec(memory_space=pltpu.SMEM)


def dot(a, b):
    return jnp.dot(a, b, preferred_element_type=F32)


def nearest(values):
    return values - jnp.floor(values * INVERSE + 0.5) * MODULUS


def centred(values):
    return jnp.where(values > 32760.0, values - MODULUS, values)


def limbs(values):
    high = jnp.floor(values * (1.0 / 256.0) + 0.5)
    return high.astype(BF16), (values - high * 256.0).astype(BF16)


def subtract_product(base, left, right):
    (a_hi, a_lo), (b_hi, b_lo) = left, right
    cross = nearest(nearest(dot(a_hi, b_lo)) + dot(a_lo, b_hi))
    upper = nearest(256.0 * cross + 15.0 * nearest(dot(a_hi, b_hi)))
    return nearest(base - upper - dot(a_lo, b_lo))


OTHERS = [(1, 1, 0), (3, 0, 0), (3, 1, 0), (1, 0, 0), (2, 1, 0), (2, 0, 0), (0, 1, 0),
          (1, 1, 1), (3, 0, 1), (3, 1, 1), (1, 0, 1), (2, 1, 1), (2, 0, 1), (0, 1, 1), (0, 0, 1)]
SOURCES = [(3, 0), (1, 0), (0, 1), (2, 0), (3, 1), (1, 1), (2, 1)]
LEFT, RIGHT, PARTNER, FAR = 0, 1, 2, 3
SPANS = [512, 2560, 2048, 1536, 1024, 512]
GROUPS = len(SPANS)
CROSS = (3,)
LINES = 48
BLOCK = 512


def exchange_kernel(
    wanted, flags, dest_ref, thin_ref, piv_ref, strip_ref, r_hbm, big_hbm,
    g,
    lines, rows, thin, ext, ext_out, tile, tile_sum, tile_in, low, hi_ref, lo_ref, pick_ref, r_ref, big_ref,
    tile_s, tile_r, low_s, low_r, low_z, low_over_r, ext_y, ext_in, row_s, row_r, ext_s, ext_r, ag_s, ag_r, core_r, ag_l, row_l, ext_l, in_l, big_l,
):
    r, c = lax.axis_index("row"), lax.axis_index("col")
    x, h, core = r // 4, lax.rem(r // 2, 2), lax.rem(r, 2)
    plane, y = c // 4, lax.rem(c, 4)

    def columns(j):
        return pl.ds(sum(SPANS[:j]), SPANS[j])

    def thin_in(j):
        return pltpu.make_async_copy(thin_ref.at[:, columns(j)], thin.at[:, columns(j)], in_l.at[j])

    constants = [
        pltpu.make_async_copy(r_hbm, r_ref, big_l.at[0]),
        pltpu.make_async_copy(big_hbm, big_ref, big_l.at[1]),
    ]
    for j in range(GROUPS):
        thin_in(j).start()
    for copy in constants:
        copy.start()

    def peer(dx, dh, dc):
        return lax.rem(x + dx, 4) * 4 + lax.rem(h + dh, 2) * 2 + lax.rem(core + dc, 2)

    other = peer(0, 0, 1)
    across_z = lax.rem(c + 4, 8)

    def along_y(k):
        return plane * 4 + lax.rem(y + k, 4)

    def send(src, dst, ssem, rsem, row, col=c):
        return pltpu.make_async_remote_copy(
            src_ref=src, dst_ref=dst, send_sem=ssem, recv_sem=rsem, device_id=(row, col), device_id_type=MESH
        )

    def took(ref, sem):
        pltpu.make_async_copy(ref, ref, sem).wait()

    barrier = pltpu.get_barrier_semaphore()
    for off in OTHERS:
        pl.semaphore_signal(barrier, inc=1, device_id=(peer(*off), c), device_id_type=MESH)
    for col in (across_z, along_y(1), along_y(2), along_y(3)):
        pl.semaphore_signal(barrier, inc=1, device_id=(r, col), device_id_type=MESH)
    pl.semaphore_wait(barrier, len(OTHERS) + 4)

    def slab(j, row):
        return lines.at[row, :, columns(j)]

    def own(j):
        for src, dst in (
            (piv_ref.at[:, columns(j)], lines.at[r, pl.ds(0, 16), columns(j)]),
            (strip_ref.at[:, columns(j)], lines.at[r, pl.ds(16, LINES - 16), columns(j)]),
        ):
            send(src, dst, ag_s.at[j], ag_r.at[j, PARTNER], peer(0, 1, 0)).start()
            send(src, dst, ag_s.at[j], ag_r.at[j, LEFT], peer(1, 0, 0)).start()
            send(src, dst, ag_s.at[j], ag_r.at[j, RIGHT], peer(3, 0, 0)).start()
            send(src, dst, ag_s.at[j], core_r.at[j], other).start()
            pltpu.make_async_copy(src, dst, ag_l.at[j]).start()

    def source(k):
        return peer(SOURCES[k][0], SOURCES[k][1], 0)

    def onward(j, k, rsem, row):
        held = slab(j, source(k))
        send(held, held, ag_s.at[j], rsem, row).start()

    def arrived(j, k):
        took(slab(j, source(k)), ag_r.at[j, k])

    def across(j, k):
        onward(j, k, core_r.at[j], other)

    def near(j):
        odd = lax.rem(x + j, 2) == 1
        arrived(j, LEFT)
        pl.when(odd)(lambda: onward(j, LEFT, ag_r.at[j, FAR], peer(1, 0, 0)))
        across(j, LEFT)
        arrived(j, RIGHT)
        pl.when(jnp.logical_not(odd))(lambda: onward(j, RIGHT, ag_r.at[j, FAR], peer(3, 0, 0)))
        across(j, RIGHT)
        if j in CROSS:
            pl.when(odd)(lambda: onward(j, RIGHT, ag_r.at[j, 5], peer(0, 1, 0)))
            pl.when(jnp.logical_not(odd))(lambda: onward(j, LEFT, ag_r.at[j, 4], peer(0, 1, 0)))
        arrived(j, PARTNER)
        if j in CROSS:
            pl.when(odd)(lambda: onward(j, PARTNER, ag_r.at[j, 5], peer(3, 0, 0)))
            pl.when(jnp.logical_not(odd))(lambda: onward(j, PARTNER, ag_r.at[j, 4], peer(1, 0, 0)))
        else:
            onward(j, PARTNER, ag_r.at[j, 4], peer(1, 0, 0))
            onward(j, PARTNER, ag_r.at[j, 5], peer(3, 0, 0))
        across(j, PARTNER)

    def far(j):
        arrived(j, FAR)
        onward(j, FAR, ag_r.at[j, 6], peer(0, 1, 0))
        across(j, FAR)

    def last(j):
        for k in (4, 5, 6):
            arrived(j, k)
            across(j, k)

    def choose():
        wide = jnp.broadcast_to(dest_ref[...], (TILE, TILE)).astype(F32)
        earlier = lax.broadcasted_iota(jnp.int32, (TILE, TILE), 0) < lax.broadcasted_iota(jnp.int32, (TILE, TILE), 1)
        same = jnp.where(earlier & (wide == wide.T), 1.0, 0.0)
        place = dest_ref[...].astype(F32) * SLOTS + jnp.sum(same, axis=0, keepdims=True)
        slot = lax.broadcasted_iota(jnp.int32, pick_ref.shape, 0).astype(F32)
        pick_ref[...] = jnp.where(slot == place, 1.0, 0.0).astype(BF16)

    def picked(part):
        high = jnp.floor(part * (1.0 / 256.0))
        moved = 256.0 * dot(pick_ref[...], high.astype(BF16)) + dot(pick_ref[...], (part - high * 256.0).astype(BF16))
        return moved.reshape(16, SLOTS, part.shape[1])

    def flag(t):
        return flags[0, t].astype(F32)

    def fill(j):
        start = sum(SPANS[:j])

        def block(i, _):
            s = pl.ds(pl.multiple_of(start + i * BLOCK, BLOCK), BLOCK)
            first = start // TILE + i * (BLOCK // TILE)
            mask = jnp.concatenate([jnp.full((1, TILE), flag(first + t), F32) for t in range(BLOCK // TILE)], axis=1)
            rows[:, :, s] = picked(thin[:, s] * mask)
            return 0

        lax.fori_loop(0, SPANS[j] // BLOCK, block, 0)

    def rows_out(j):
        s = columns(j)
        for off in OTHERS:
            to = peer(*off)
            send(rows.at[to, :, s], g.at[r, :, s], row_s.at[j], row_r.at[j], to).start()
        pltpu.make_async_copy(rows.at[r, :, s], g.at[r, :, s], row_l.at[j]).start()

    def tile_along(k):
        there = lax.rem(y + k, 4)
        return send(tile.at[lax.rem(there, 2)], tile_in.at[k], tile_s.at[k], tile_r.at[k], r, along_y(k))

    def tile_across():
        return send(tile_sum, tile_in.at[0], tile_s.at[0], tile_r.at[0], r, across_z)

    def select():
        def one(t, found):
            s = pl.ds(pl.multiple_of(t * TILE, TILE), TILE)
            part, head = thin[:, s], piv_ref[pl.ds(0, 8), s]
            at = [jnp.where(wanted[k] == c * flags.shape[1] + t, 1.0, 0.0) for k in range(2)]
            return (
                found[0] + part * (flag(t) * at[0]),
                found[1] + part * (flag(t) * at[1]),
                found[2] + head * at[1],
            )

        none = jnp.zeros((TILE, TILE), F32)
        found = lax.fori_loop(0, flags.shape[1], one, (none, none, jnp.zeros((8, TILE), F32)))
        for k in range(2):
            tile[k, pl.ds(0, TILE), :] = found[k]
            tile[k, pl.ds(TILE, 8), :] = found[2]

    def tile_begin():
        for k in (1, 2, 3):
            tile_along(k).start()

    def tile_next():
        total = jnp.where(lax.rem(y, 2) == 0, tile[0], tile[1])
        for k in (1, 2, 3):
            tile_along(k).wait_recv()
            total = total + tile_in[k]
        tile_sum[...] = total
        tile_across().start()

    def ext_begin():
        tile_across().wait_recv()
        total = tile_sum[...] + tile_in[0]
        slots = picked(total[:TILE, :])
        ext_out[:, pl.ds(0, 8), :] = jnp.where(y < 2, slots[:, :8], slots[:, 8:])
        ext_out[:, pl.ds(8, 8), :] = jnp.broadcast_to(total[TILE:, :][None], (16, 8, TILE))
        for off in OTHERS:
            to = peer(*off)
            send(ext_out.at[to], ext.at[y, r], ext_s, ext_r, to).start()
        pltpu.make_async_copy(ext_out.at[r], ext.at[y, r], ext_l).start()

    def ext_along(k):
        return send(ext.at[y], ext.at[y], ext_y, ext_in, r, along_y(k))

    def ext_next():
        took(ext.at[y, pl.ds(0, 15)], ext_r)
        took(ext.at[y, 0], ext_l)
        for k in (1, 2, 3):
            ext_along(k).start()

    def keep(parts, at):
        for ref, part in zip((hi_ref, lo_ref), parts):
            ref[:, pl.ds(at, part.shape[1])] = part

    def kept(at):
        return hi_ref[:, pl.ds(at, TILE)], lo_ref[:, pl.ds(at, TILE)]

    zero = jnp.zeros((16 * SLOTS, 1), F32)

    def factors():
        took(ext.at[pl.ds(0, 3)], ext_in)
        for copy in constants:
            copy.wait()
        halves = [ext[k, :, :8, :] for k in range(4)]
        terms = [jnp.concatenate([halves[k], halves[k + 2]], axis=1).reshape(16 * SLOTS, TILE) for k in range(2)]
        pivot = limbs(centred(ext[0, :, 8:, :].reshape(TILE, TILE)))
        first = limbs(-subtract_product(zero, limbs(centred(terms[0])), limbs(centred(r_ref[0]))))
        second = subtract_product(terms[1], first, pivot)
        second = limbs(-subtract_product(zero, limbs(second), limbs(centred(r_ref[1]))))
        keep(first, 0)
        keep(second, TILE)

    def quarter(k):
        return low.at[pl.ds(k * (4 * SLOTS), 4 * SLOTS)]

    def low_out(k):
        return send(low, low, low_s.at[k - 1], low_r, r, k)

    def low_over():
        return send(quarter(y), quarter(y), low_z, low_over_r, r, across_z)

    def low_along(k):
        return send(quarter(y), quarter(y), low_s.at[k - 1], low_r, r, along_y(k))

    def lower_begin():
        @pl.when(c == 0)
        def _():
            base = g[:, :, :PANEL].reshape(16 * SLOTS, PANEL)
            for k in range(2):
                part = lines[:, 8 * k : 8 * k + 8, :PANEL].reshape(TILE, PANEL)
                base = subtract_product(base, kept(k * TILE), limbs(centred(part)))
            low[...] = -subtract_product(zero, limbs(base), limbs(centred(big_ref[...])))
            for k in (1, 3, 2):
                low_out(k).start()

    def lower_next():
        @pl.when((plane == 0) & (y != 0))
        def _():
            low_out(1).wait_recv()

        @pl.when(plane == 0)
        def _():
            low_over().start()

        @pl.when(plane == 1)
        def _():
            low_over().wait_recv()
            for k in (1, 3, 2):
                low_along(k).start()

    def lower_end():
        @pl.when(plane == 1)
        def _():
            took(low.at[pl.ds(0, 12 * SLOTS)], low_r)

        keep(limbs(low[...]), 2 * TILE)

    def complete(j):
        s = columns(j)
        took(lines.at[pl.ds(0, 8), :, s], core_r.at[j])
        took(slab(j, r), ag_l.at[j])
        took(g.at[pl.ds(0, 15), :, s], row_r.at[j])
        took(g.at[0, :, s], row_l.at[j])

    def compute(j):
        start = sum(SPANS[:j])

        def block(i, _):
            s = pl.ds(pl.multiple_of(start + i * BLOCK, BLOCK), BLOCK)
            held = lines[:, :, s]
            inner = jnp.concatenate(
                [held[:, 0:8].reshape(TILE, BLOCK), held[:, 8:16].reshape(TILE, BLOCK),
                 held[:, 16:].reshape(PANEL, BLOCK)], axis=0
            )
            base = g[:, :, s].reshape(16 * SLOTS, BLOCK)
            result = subtract_product(base, (hi_ref[...], lo_ref[...]), limbs(centred(inner)))
            result = jnp.where(result < 0.0, result + MODULUS, result) * INVERSE
            g[:, :, s] = result.reshape(16, SLOTS, BLOCK)
            return 0

        lax.fori_loop(0, SPANS[j] // BLOCK, block, 0)

    own(0)
    own(1)
    choose()
    for j in range(GROUPS):
        thin_in(j).wait()
    select()
    tile_begin()
    fill(0)
    rows_out(0)
    near(0)
    tile_next()
    far(0)
    ext_begin()
    own(2)
    fill(1)
    rows_out(1)
    last(0)
    ext_next()
    own(3)
    fill(2)
    near(1)
    factors()
    complete(0)
    lower_begin()
    rows_out(2)
    own(4)
    fill(3)
    near(2)
    far(1)
    lower_next()
    own(5)
    rows_out(3)
    fill(4)
    fill(5)
    near(3)
    far(2)
    last(1)
    lower_end()
    rows_out(4)
    near(4)
    compute(0)
    far(3)
    last(2)
    rows_out(5)
    near(5)
    complete(1)
    compute(1)
    far(4)
    last(3)
    complete(2)
    compute(2)
    far(5)
    last(4)
    complete(3)
    compute(3)
    last(5)
    complete(4)
    compute(4)
    complete(5)
    compute(5)

    for j in range(GROUPS):
        took(lines.at[pl.ds(0, 15), :, columns(j)], ag_s.at[j])
        took(g.at[pl.ds(0, 15), :, columns(j)], row_s.at[j])
    took(ext.at[0, pl.ds(0, 15)], ext_s)
    took(ext.at[pl.ds(0, 3)], ext_y)
    tile_across().wait_send()
    for k in (1, 2, 3):
        tile_along(k).wait_send()

    @pl.when(c == 0)
    def _():
        for k in (1, 2, 3):
            low_out(k).wait_send()

    @pl.when(plane == 0)
    def _():
        low_over().wait_send()

    @pl.when(plane == 1)
    def _():
        for k in (1, 2, 3):
            low_along(k).wait_send()


def exchange(wanted, flags, dest, thin, piv, strip, recips, big):
    width = thin.shape[1]
    dma = pltpu.SemaphoreType.DMA
    head = (TILE + 8, TILE)
    return pl.pallas_call(
        exchange_kernel,
        in_specs=[SM, SM, VM, ANY, VM, ANY, ANY, ANY],
        out_specs=VM,
        out_shape=pltpu.VMEM((16, SLOTS, width), F32),
        scratch_shapes=[
            pltpu.VMEM((16, LINES, width), F32),
            pltpu.VMEM((16, SLOTS, width), F32),
            pltpu.VMEM(thin.shape, F32),
            pltpu.VMEM((4, 16, SLOTS, TILE), F32),
            pltpu.VMEM((16, SLOTS, TILE), F32),
            pltpu.VMEM((2,) + head, F32),
            pltpu.VMEM(head, F32),
            pltpu.VMEM((4,) + head, F32),
            pltpu.VMEM((16 * SLOTS, PANEL), F32),
            pltpu.VMEM((16 * SLOTS, 2 * TILE + PANEL), BF16),
            pltpu.VMEM((16 * SLOTS, 2 * TILE + PANEL), BF16),
            pltpu.VMEM((16 * SLOTS, TILE), BF16),
            pltpu.VMEM(recips.shape, F32),
            pltpu.VMEM(big.shape, F32),
            dma((4,)), dma((4,)), dma((3,)), dma(()), dma(()), dma(()), dma(()), dma(()),
            dma((GROUPS,)), dma((GROUPS,)), dma(()), dma(()),
            dma((GROUPS,)), dma((GROUPS, 7)), dma((GROUPS,)),
            dma((GROUPS,)), dma((GROUPS,)), dma(()), dma((GROUPS,)), dma((2,)),
        ],
        name="exchange",
        compiler_params=pltpu.CompilerParams(
            collective_id=0, has_side_effects=True, vmem_limit_bytes=52 << 20
        ),
    )(wanted, flags, dest, thin, piv, strip, recips, big)


def local(thin, flags, tiles, pivots, recips, dest, strip, big):
    width = thin.shape[1]
    out = exchange(tiles, flags, dest[None, :], thin, pivots.reshape(16, width), strip, recips, big)
    return out.reshape(16 * SLOTS, width)


def solution(mesh):
    return jax.shard_map(
        local,
        mesh=mesh,
        in_specs=(
            P("row", "col"),
            P("row", "col"),
            P(),
            P(None, "row", "col"),
            P(),
            P("row"),
            P("row", "col"),
            P(),
        ),
        out_specs=P("row", "col"),
        check_vma=False,
    )
```

```python
import functools

import jax
import jax.numpy as jnp
from jax import lax
from jax.experimental import pallas as pl
from jax.experimental.pallas import tpu as pltpu
from jax.sharding import PartitionSpec as P

TILE = 128
PANEL = 512
SLOTS = 16
MODULUS = 65521.0
INVERSE = 1.0 / 65521.0
MESH = pl.DeviceIdType.MESH
F32, BF16 = jnp.float32, jnp.bfloat16
ANY = pl.BlockSpec(memory_space=pl.ANY)
VM = pl.BlockSpec(memory_space=pltpu.VMEM)
SM = pl.BlockSpec(memory_space=pltpu.SMEM)


def dot(a, b):
    return jnp.dot(a, b, preferred_element_type=F32)


def nearest(values):
    return values - jnp.floor(values * INVERSE + 0.5) * MODULUS


def centred(values):
    return jnp.where(values > 32760.0, values - MODULUS, values)


def limbs(values):
    high = jnp.floor(values * (1.0 / 256.0) + 0.5)
    return high.astype(BF16), (values - high * 256.0).astype(BF16)


def product(left, right):
    (a_hi, a_lo), (b_hi, b_lo) = left, right
    cross = nearest(nearest(dot(a_hi, b_lo)) + dot(a_lo, b_hi))
    upper = nearest(256.0 * cross + 15.0 * nearest(dot(a_hi, b_hi)))
    return upper + dot(a_lo, b_lo)


def subtract_product(base, left, right):
    return nearest(base - product(left, right))


OTHERS = [(1, 1, 0), (3, 0, 0), (3, 1, 0), (1, 0, 0), (2, 1, 0), (2, 0, 0), (0, 1, 0),
          (1, 1, 1), (3, 0, 1), (3, 1, 1), (1, 0, 1), (2, 1, 1), (2, 0, 1), (0, 1, 1), (0, 0, 1)]
SOURCES = [(3, 0), (1, 0), (0, 1), (2, 0), (3, 1), (1, 1), (2, 1)]
LEFT, RIGHT, PARTNER, FAR = 0, 1, 2, 3
SPANS = [512, 2560, 2048, 1536, 1024, 512]
GROUPS = len(SPANS)
CROSS = (3,)
LATE = 3
LINES = 48
BLOCK = 512


def exchange_kernel(
    wanted, flags, dest_ref, thin_ref, piv_ref, strip_ref, r_hbm, big_hbm,
    g,
    lines, rows, thin, ready, ext, ext_out, tile, tile_sum, tile_in, low, hi_ref, lo_ref, pick_ref, r_ref, big_ref,
    tile_s, tile_r, low_s, low_r, low_z, low_over_r, ext_y, ext_in, row_s, row_r, ext_s, ext_r, ag_s, ag_r, core_r, ag_l, row_l, ext_l, in_l, big_l,
):
    r, c = lax.axis_index("row"), lax.axis_index("col")
    x, h, core = r // 4, lax.rem(r // 2, 2), lax.rem(r, 2)
    plane, y = c // 4, lax.rem(c, 4)

    def columns(j):
        return pl.ds(sum(SPANS[:j]), SPANS[j])

    def thin_in(j):
        return pltpu.make_async_copy(thin_ref.at[:, columns(j)], thin.at[:, columns(j)], in_l.at[j])

    constants = [
        pltpu.make_async_copy(r_hbm, r_ref, big_l.at[0]),
        pltpu.make_async_copy(big_hbm, big_ref, big_l.at[1]),
    ]
    for j in range(GROUPS):
        thin_in(j).start()
    for copy in constants:
        copy.start()

    def peer(dx, dh, dc):
        return lax.rem(x + dx, 4) * 4 + lax.rem(h + dh, 2) * 2 + lax.rem(core + dc, 2)

    other = peer(0, 0, 1)
    across_z = lax.rem(c + 4, 8)

    def along_y(k):
        return plane * 4 + lax.rem(y + k, 4)

    def send(src, dst, ssem, rsem, row, col=c):
        return pltpu.make_async_remote_copy(
            src_ref=src, dst_ref=dst, send_sem=ssem, recv_sem=rsem, device_id=(row, col), device_id_type=MESH
        )

    def took(ref, sem):
        pltpu.make_async_copy(ref, ref, sem).wait()

    barrier = pltpu.get_barrier_semaphore()
    for off in OTHERS:
        pl.semaphore_signal(barrier, inc=1, device_id=(peer(*off), c), device_id_type=MESH)
    for col in (across_z, along_y(1), along_y(2), along_y(3)):
        pl.semaphore_signal(barrier, inc=1, device_id=(r, col), device_id_type=MESH)
    pl.semaphore_wait(barrier, len(OTHERS) + 4)

    def slab(j, row):
        return lines.at[row, :, columns(j)]

    def own(j):
        for src, dst in (
            (piv_ref.at[:, columns(j)], lines.at[r, pl.ds(0, 16), columns(j)]),
            (strip_ref.at[:, columns(j)], lines.at[r, pl.ds(16, LINES - 16), columns(j)]),
        ):
            send(src, dst, ag_s.at[j], ag_r.at[j, PARTNER], peer(0, 1, 0)).start()
            send(src, dst, ag_s.at[j], ag_r.at[j, LEFT], peer(1, 0, 0)).start()
            send(src, dst, ag_s.at[j], ag_r.at[j, RIGHT], peer(3, 0, 0)).start()
            send(src, dst, ag_s.at[j], core_r.at[j], other).start()
            pltpu.make_async_copy(src, dst, ag_l.at[j]).start()

    def source(k):
        return peer(SOURCES[k][0], SOURCES[k][1], 0)

    def onward(j, k, rsem, row):
        held = slab(j, source(k))
        send(held, held, ag_s.at[j], rsem, row).start()

    def arrived(j, k):
        took(slab(j, source(k)), ag_r.at[j, k])

    def across(j, k):
        onward(j, k, core_r.at[j], other)

    def near(j):
        odd = lax.rem(x + j, 2) == 1
        arrived(j, LEFT)
        pl.when(odd)(lambda: onward(j, LEFT, ag_r.at[j, FAR], peer(1, 0, 0)))
        across(j, LEFT)
        arrived(j, RIGHT)
        pl.when(jnp.logical_not(odd))(lambda: onward(j, RIGHT, ag_r.at[j, FAR], peer(3, 0, 0)))
        across(j, RIGHT)
        if j in CROSS:
            pl.when(odd)(lambda: onward(j, RIGHT, ag_r.at[j, 5], peer(0, 1, 0)))
            pl.when(jnp.logical_not(odd))(lambda: onward(j, LEFT, ag_r.at[j, 4], peer(0, 1, 0)))
        arrived(j, PARTNER)
        if j in CROSS:
            pl.when(odd)(lambda: onward(j, PARTNER, ag_r.at[j, 5], peer(3, 0, 0)))
            pl.when(jnp.logical_not(odd))(lambda: onward(j, PARTNER, ag_r.at[j, 4], peer(1, 0, 0)))
        else:
            onward(j, PARTNER, ag_r.at[j, 4], peer(1, 0, 0))
            onward(j, PARTNER, ag_r.at[j, 5], peer(3, 0, 0))
        across(j, PARTNER)

    def far(j):
        arrived(j, FAR)
        onward(j, FAR, ag_r.at[j, 6], peer(0, 1, 0))
        across(j, FAR)

    def last(j):
        for k in (4, 5, 6):
            arrived(j, k)
            across(j, k)

    def choose():
        wide = jnp.broadcast_to(dest_ref[...], (TILE, TILE)).astype(F32)
        earlier = lax.broadcasted_iota(jnp.int32, (TILE, TILE), 0) < lax.broadcasted_iota(jnp.int32, (TILE, TILE), 1)
        same = jnp.where(earlier & (wide == wide.T), 1.0, 0.0)
        place = dest_ref[...].astype(F32) * SLOTS + jnp.sum(same, axis=0, keepdims=True)
        slot = lax.broadcasted_iota(jnp.int32, pick_ref.shape, 0).astype(F32)
        pick_ref[...] = jnp.where(slot == place, 1.0, 0.0).astype(BF16)

    def picked(part):
        high = jnp.floor(part * (1.0 / 256.0))
        moved = 256.0 * dot(pick_ref[...], high.astype(BF16)) + dot(pick_ref[...], (part - high * 256.0).astype(BF16))
        return moved.reshape(16, SLOTS, part.shape[1])

    def flag(t):
        return flags[0, t].astype(F32)

    def fill(j):
        start = sum(SPANS[:j])

        def block(i, _):
            s = pl.ds(pl.multiple_of(start + i * BLOCK, BLOCK), BLOCK)
            first = start // TILE + i * (BLOCK // TILE)
            mask = jnp.concatenate([jnp.full((1, TILE), flag(first + t), F32) for t in range(BLOCK // TILE)], axis=1)
            rows[:, :, s] = picked(thin[:, s] * mask)
            return 0

        lax.fori_loop(0, SPANS[j] // BLOCK, block, 0)

    def rows_out(j):
        s = columns(j)
        for off in OTHERS:
            to = peer(*off)
            send(rows.at[to, :, s], g.at[r, :, s], row_s.at[j], row_r.at[j], to).start()
        pltpu.make_async_copy(rows.at[r, :, s], g.at[r, :, s], row_l.at[j]).start()

    def tile_along(k):
        there = lax.rem(y + k, 4)
        return send(tile.at[lax.rem(there, 2)], tile_in.at[k], tile_s.at[k], tile_r.at[k], r, along_y(k))

    def tile_across():
        return send(tile_sum, tile_in.at[0], tile_s.at[0], tile_r.at[0], r, across_z)

    def select():
        def one(t, found):
            s = pl.ds(pl.multiple_of(t * TILE, TILE), TILE)
            part, head = thin[:, s], piv_ref[pl.ds(0, 8), s]
            at = [jnp.where(wanted[k] == c * flags.shape[1] + t, 1.0, 0.0) for k in range(2)]
            return (
                found[0] + part * (flag(t) * at[0]),
                found[1] + part * (flag(t) * at[1]),
                found[2] + head * at[1],
            )

        none = jnp.zeros((TILE, TILE), F32)
        found = lax.fori_loop(0, flags.shape[1], one, (none, none, jnp.zeros((8, TILE), F32)))
        for k in range(2):
            tile[k, pl.ds(0, TILE), :] = found[k]
            tile[k, pl.ds(TILE, 8), :] = found[2]

    def tile_begin():
        for k in (1, 2, 3):
            tile_along(k).start()

    def tile_next():
        total = jnp.where(lax.rem(y, 2) == 0, tile[0], tile[1])
        for k in (1, 2, 3):
            tile_along(k).wait_recv()
            total = total + tile_in[k]
        tile_sum[...] = total
        tile_across().start()

    def ext_begin():
        tile_across().wait_recv()
        total = tile_sum[...] + tile_in[0]
        slots = picked(total[:TILE, :])
        ext_out[:, pl.ds(0, 8), :] = jnp.where(y < 2, slots[:, :8], slots[:, 8:])
        ext_out[:, pl.ds(8, 8), :] = jnp.broadcast_to(total[TILE:, :][None], (16, 8, TILE))
        for off in OTHERS:
            to = peer(*off)
            send(ext_out.at[to], ext.at[y, r], ext_s, ext_r, to).start()
        pltpu.make_async_copy(ext_out.at[r], ext.at[y, r], ext_l).start()

    def ext_along(k):
        return send(ext.at[y], ext.at[y], ext_y, ext_in, r, along_y(k))

    def ext_next():
        took(ext.at[y, pl.ds(0, 15)], ext_r)
        took(ext.at[y, 0], ext_l)
        for k in (1, 2, 3):
            ext_along(k).start()

    def keep(parts, at):
        for ref, part in zip((hi_ref, lo_ref), parts):
            ref[:, pl.ds(at, part.shape[1])] = part

    def kept(at):
        return hi_ref[:, pl.ds(at, TILE)], lo_ref[:, pl.ds(at, TILE)]

    zero = jnp.zeros((16 * SLOTS, 1), F32)

    def factors():
        took(ext.at[pl.ds(0, 3)], ext_in)
        for copy in constants:
            copy.wait()
        halves = [ext[k, :, :8, :] for k in range(4)]
        terms = [jnp.concatenate([halves[k], halves[k + 2]], axis=1).reshape(16 * SLOTS, TILE) for k in range(2)]
        pivot = limbs(centred(ext[0, :, 8:, :].reshape(TILE, TILE)))
        first = limbs(-subtract_product(zero, limbs(centred(terms[0])), limbs(centred(r_ref[0]))))
        second = subtract_product(terms[1], first, pivot)
        second = limbs(-subtract_product(zero, limbs(second), limbs(centred(r_ref[1]))))
        keep(first, 0)
        keep(second, TILE)

    def quarter(k):
        return low.at[pl.ds(k * (4 * SLOTS), 4 * SLOTS)]

    def low_out(k):
        return send(low, low, low_s.at[k - 1], low_r, r, k)

    def low_over():
        return send(quarter(y), quarter(y), low_z, low_over_r, r, across_z)

    def low_along(k):
        return send(quarter(y), quarter(y), low_s.at[k - 1], low_r, r, along_y(k))

    def lower_begin():
        @pl.when(c == 0)
        def _():
            base = g[:, :, :PANEL].reshape(16 * SLOTS, PANEL)
            for k in range(2):
                part = lines[:, 8 * k : 8 * k + 8, :PANEL].reshape(TILE, PANEL)
                base = subtract_product(base, kept(k * TILE), limbs(centred(part)))
            low[...] = -subtract_product(zero, limbs(base), limbs(centred(big_ref[...])))
            for k in (1, 3, 2):
                low_out(k).start()

    def lower_next():
        @pl.when((plane == 0) & (y != 0))
        def _():
            low_out(1).wait_recv()

        @pl.when(plane == 0)
        def _():
            low_over().start()

        @pl.when(plane == 1)
        def _():
            low_over().wait_recv()
            for k in (1, 3, 2):
                low_along(k).start()

    def lower_end():
        @pl.when(plane == 1)
        def _():
            took(low.at[pl.ds(0, 12 * SLOTS)], low_r)

        keep(limbs(low[...]), 2 * TILE)

    def lines_done(j):
        took(lines.at[pl.ds(0, 8), :, columns(j)], core_r.at[j])
        took(slab(j, r), ag_l.at[j])

    def rows_done(j):
        took(g.at[pl.ds(0, 15), :, columns(j)], row_r.at[j])
        took(g.at[0, :, columns(j)], row_l.at[j])

    def each_block(j, body):
        def block(i, _):
            body(pl.multiple_of(sum(SPANS[:j]) + i * BLOCK, BLOCK))
            return 0

        lax.fori_loop(0, SPANS[j] // BLOCK, block, 0)

    def ready_at(at):
        return pl.ds(pl.multiple_of(at - sum(SPANS[:LATE]), BLOCK), BLOCK)

    def put(s, amount):
        result = nearest(g[:, :, s].reshape(16 * SLOTS, BLOCK) - amount)
        result = jnp.where(result < 0.0, result + MODULUS, result) * INVERSE
        g[:, :, s] = result.reshape(16, SLOTS, BLOCK)

    def compute(j, early=False):
        def body(at):
            s = pl.ds(at, BLOCK)
            held = lines[:, :, s]
            inner = jnp.concatenate(
                [held[:, 0:8].reshape(TILE, BLOCK), held[:, 8:16].reshape(TILE, BLOCK),
                 held[:, 16:].reshape(PANEL, BLOCK)], axis=0
            )
            amount = product((hi_ref[...], lo_ref[...]), limbs(centred(inner)))
            if early:
                ready[:, ready_at(at)] = amount
            else:
                put(s, amount)

        each_block(j, body)

    def finish(j):
        each_block(j, lambda at: put(pl.ds(at, BLOCK), ready[:, ready_at(at)]))

    own(0)
    own(1)
    choose()
    for j in range(GROUPS):
        thin_in(j).wait()
    select()
    tile_begin()
    fill(0)
    rows_out(0)
    near(0)
    tile_next()
    far(0)
    ext_begin()
    own(2)
    fill(1)
    rows_out(1)
    last(0)
    ext_next()
    own(3)
    fill(2)
    near(1)
    factors()
    lines_done(0)
    rows_done(0)
    lower_begin()
    rows_out(2)
    own(4)
    fill(3)
    near(2)
    far(1)
    lower_next()
    own(5)
    fill(4)
    fill(5)
    near(3)
    rows_out(3)
    far(2)
    last(1)
    lower_end()
    near(4)
    rows_out(4)
    compute(0)
    far(3)
    last(2)
    near(5)
    rows_out(5)
    lines_done(1)
    rows_done(1)
    compute(1)
    far(4)
    last(3)
    lines_done(2)
    rows_done(2)
    compute(2)
    far(5)
    last(4)
    lines_done(3)
    compute(3, early=True)
    lines_done(4)
    compute(4, early=True)
    last(5)
    lines_done(5)
    compute(5, early=True)
    rows_done(3)
    finish(3)
    rows_done(4)
    finish(4)
    rows_done(5)
    finish(5)

    for j in range(GROUPS):
        took(lines.at[pl.ds(0, 15), :, columns(j)], ag_s.at[j])
        took(g.at[pl.ds(0, 15), :, columns(j)], row_s.at[j])
    took(ext.at[0, pl.ds(0, 15)], ext_s)
    took(ext.at[pl.ds(0, 3)], ext_y)
    tile_across().wait_send()
    for k in (1, 2, 3):
        tile_along(k).wait_send()

    @pl.when(c == 0)
    def _():
        for k in (1, 2, 3):
            low_out(k).wait_send()

    @pl.when(plane == 0)
    def _():
        low_over().wait_send()

    @pl.when(plane == 1)
    def _():
        for k in (1, 2, 3):
            low_along(k).wait_send()


def exchange(wanted, flags, dest, thin, piv, strip, recips, big):
    width = thin.shape[1]
    dma = pltpu.SemaphoreType.DMA
    head = (TILE + 8, TILE)
    return pl.pallas_call(
        exchange_kernel,
        in_specs=[SM, SM, VM, ANY, VM, ANY, ANY, ANY],
        out_specs=VM,
        out_shape=pltpu.VMEM((16, SLOTS, width), F32),
        scratch_shapes=[
            pltpu.VMEM((16, LINES, width), F32),
            pltpu.VMEM((16, SLOTS, width), F32),
            pltpu.VMEM(thin.shape, F32),
            pltpu.VMEM((16 * SLOTS, sum(SPANS[LATE:])), F32),
            pltpu.VMEM((4, 16, SLOTS, TILE), F32),
            pltpu.VMEM((16, SLOTS, TILE), F32),
            pltpu.VMEM((2,) + head, F32),
            pltpu.VMEM(head, F32),
            pltpu.VMEM((4,) + head, F32),
            pltpu.VMEM((16 * SLOTS, PANEL), F32),
            pltpu.VMEM((16 * SLOTS, 2 * TILE + PANEL), BF16),
            pltpu.VMEM((16 * SLOTS, 2 * TILE + PANEL), BF16),
            pltpu.VMEM((16 * SLOTS, TILE), BF16),
            pltpu.VMEM(recips.shape, F32),
            pltpu.VMEM(big.shape, F32),
            dma((4,)), dma((4,)), dma((3,)), dma(()), dma(()), dma(()), dma(()), dma(()),
            dma((GROUPS,)), dma((GROUPS,)), dma(()), dma(()),
            dma((GROUPS,)), dma((GROUPS, 7)), dma((GROUPS,)),
            dma((GROUPS,)), dma((GROUPS,)), dma(()), dma((GROUPS,)), dma((2,)),
        ],
        name="exchange",
        compiler_params=pltpu.CompilerParams(
            collective_id=0, has_side_effects=True, vmem_limit_bytes=52 << 20
        ),
    )(wanted, flags, dest, thin, piv, strip, recips, big)


def local(thin, flags, tiles, pivots, recips, dest, strip, big):
    width = thin.shape[1]
    out = exchange(tiles, flags, dest[None, :], thin, pivots.reshape(16, width), strip, recips, big)
    return out.reshape(16 * SLOTS, width)


def solution(mesh):
    return jax.shard_map(
        local,
        mesh=mesh,
        in_specs=(
            P("row", "col"),
            P("row", "col"),
            P(),
            P(None, "row", "col"),
            P(),
            P("row"),
            P("row", "col"),
            P(),
        ),
        out_specs=P("row", "col"),
        check_vma=False,
    )
```

```python
import functools

import jax
import jax.numpy as jnp
from jax import lax
from jax.experimental import pallas as pl
from jax.experimental.pallas import tpu as pltpu
from jax.sharding import PartitionSpec as P

TILE = 128
PANEL = 512
SLOTS = 16
MODULUS = 65521.0
INVERSE = 1.0 / 65521.0
MESH = pl.DeviceIdType.MESH
F32, BF16 = jnp.float32, jnp.bfloat16
ANY = pl.BlockSpec(memory_space=pl.ANY)
VM = pl.BlockSpec(memory_space=pltpu.VMEM)
SM = pl.BlockSpec(memory_space=pltpu.SMEM)


def dot(a, b):
    return jnp.dot(a, b, preferred_element_type=F32)


def nearest(values):
    return values - jnp.floor(values * INVERSE + 0.5) * MODULUS


def centred(values):
    return jnp.where(values > 32760.0, values - MODULUS, values)


def limbs(values):
    high = jnp.floor(values * (1.0 / 256.0) + 0.5)
    return high.astype(BF16), (values - high * 256.0).astype(BF16)


def product(left, right):
    (a_hi, a_lo), (b_hi, b_lo) = left, right
    cross = nearest(nearest(dot(a_hi, b_lo)) + dot(a_lo, b_hi))
    upper = nearest(256.0 * cross + 15.0 * nearest(dot(a_hi, b_hi)))
    return upper + dot(a_lo, b_lo)


def subtract_product(base, left, right):
    return nearest(base - product(left, right))


OTHERS = [(1, 1, 0), (3, 0, 0), (3, 1, 0), (1, 0, 0), (2, 1, 0), (2, 0, 0), (0, 1, 0),
          (1, 1, 1), (3, 0, 1), (3, 1, 1), (1, 0, 1), (2, 1, 1), (2, 0, 1), (0, 1, 1), (0, 0, 1)]
SOURCES = [(3, 0), (1, 0), (0, 1), (2, 0), (3, 1), (1, 1), (2, 1)]
LEFT, RIGHT, PARTNER, FAR = 0, 1, 2, 3
SPANS = [512, 2560, 2048, 1536, 1024, 512]
GROUPS = len(SPANS)
CROSS = (3,)
LATE = 3
LINES = 48
BLOCK = 512


def residue(moved, amount):
    result = nearest(moved.reshape(amount.shape) - amount)
    return (jnp.where(result < 0.0, result + MODULUS, result) * INVERSE).reshape(moved.shape)


def close_kernel(g, ready, out_ref, done, sems):
    copies = []

    def leave(src, s):
        copies.append(pltpu.make_async_copy(src, out_ref.at[:, :, s], sems.at[len(copies)]))
        copies[-1].start()

    early = sum(SPANS[:LATE])
    for j in range(LATE):
        s = pl.ds(sum(SPANS[:j]), SPANS[j])
        leave(g.at[:, :, s], s)
    for at in range(0, sum(SPANS[LATE:]), BLOCK):
        s = pl.ds(early + at, BLOCK)
        done[:, :, pl.ds(at, BLOCK)] = residue(g[:, :, s], ready[:, pl.ds(at, BLOCK)])
        leave(done.at[:, :, pl.ds(at, BLOCK)], s)
    for copy in copies:
        copy.wait()


def close(g, ready):
    late = ready.shape[1]
    return pl.pallas_call(
        close_kernel,
        in_specs=[VM, VM],
        out_specs=ANY,
        out_shape=jax.ShapeDtypeStruct(g.shape, F32),
        scratch_shapes=[
            pltpu.VMEM((16, SLOTS, late), F32),
            pltpu.SemaphoreType.DMA((LATE + late // BLOCK,)),
        ],
        name="close",
        compiler_params=pltpu.CompilerParams(vmem_limit_bytes=16 << 20),
    )(g, ready)


def exchange_kernel(
    wanted, flags, dest_ref, thin_ref, piv_ref, strip_ref, r_hbm, big_hbm,
    g, ready,
    lines, rows, thin, ext, ext_out, tile, tile_sum, tile_in, low, hi_ref, lo_ref, pick_ref, r_ref, big_ref,
    tile_s, tile_r, low_s, low_r, low_z, low_over_r, ext_y, ext_in, row_s, row_r, ext_s, ext_r, ag_s, ag_r, core_r, ag_l, row_l, ext_l, in_l, big_l,
):
    r, c = lax.axis_index("row"), lax.axis_index("col")
    x, h, core = r // 4, lax.rem(r // 2, 2), lax.rem(r, 2)
    plane, y = c // 4, lax.rem(c, 4)

    def columns(j):
        return pl.ds(sum(SPANS[:j]), SPANS[j])

    def thin_in(j):
        return pltpu.make_async_copy(thin_ref.at[:, columns(j)], thin.at[:, columns(j)], in_l.at[j])

    constants = [
        pltpu.make_async_copy(r_hbm, r_ref, big_l.at[0]),
        pltpu.make_async_copy(big_hbm, big_ref, big_l.at[1]),
    ]
    for j in range(GROUPS):
        thin_in(j).start()
    for copy in constants:
        copy.start()

    def peer(dx, dh, dc):
        return lax.rem(x + dx, 4) * 4 + lax.rem(h + dh, 2) * 2 + lax.rem(core + dc, 2)

    other = peer(0, 0, 1)
    across_z = lax.rem(c + 4, 8)

    def along_y(k):
        return plane * 4 + lax.rem(y + k, 4)

    def send(src, dst, ssem, rsem, row, col=c):
        return pltpu.make_async_remote_copy(
            src_ref=src, dst_ref=dst, send_sem=ssem, recv_sem=rsem, device_id=(row, col), device_id_type=MESH
        )

    def took(ref, sem):
        pltpu.make_async_copy(ref, ref, sem).wait()

    barrier = pltpu.get_barrier_semaphore()
    for off in OTHERS:
        pl.semaphore_signal(barrier, inc=1, device_id=(peer(*off), c), device_id_type=MESH)
    for col in (across_z, along_y(1), along_y(2), along_y(3)):
        pl.semaphore_signal(barrier, inc=1, device_id=(r, col), device_id_type=MESH)
    pl.semaphore_wait(barrier, len(OTHERS) + 4)

    def slab(j, row):
        return lines.at[row, :, columns(j)]

    def own(j):
        for src, dst in (
            (piv_ref.at[:, columns(j)], lines.at[r, pl.ds(0, 16), columns(j)]),
            (strip_ref.at[:, columns(j)], lines.at[r, pl.ds(16, LINES - 16), columns(j)]),
        ):
            send(src, dst, ag_s.at[j], ag_r.at[j, PARTNER], peer(0, 1, 0)).start()
            send(src, dst, ag_s.at[j], ag_r.at[j, LEFT], peer(1, 0, 0)).start()
            send(src, dst, ag_s.at[j], ag_r.at[j, RIGHT], peer(3, 0, 0)).start()
            send(src, dst, ag_s.at[j], core_r.at[j], other).start()
            pltpu.make_async_copy(src, dst, ag_l.at[j]).start()

    def source(k):
        return peer(SOURCES[k][0], SOURCES[k][1], 0)

    def onward(j, k, rsem, row):
        held = slab(j, source(k))
        send(held, held, ag_s.at[j], rsem, row).start()

    def arrived(j, k):
        took(slab(j, source(k)), ag_r.at[j, k])

    def across(j, k):
        onward(j, k, core_r.at[j], other)

    def near(j):
        odd = lax.rem(x + j, 2) == 1
        arrived(j, LEFT)
        pl.when(odd)(lambda: onward(j, LEFT, ag_r.at[j, FAR], peer(1, 0, 0)))
        across(j, LEFT)
        arrived(j, RIGHT)
        pl.when(jnp.logical_not(odd))(lambda: onward(j, RIGHT, ag_r.at[j, FAR], peer(3, 0, 0)))
        across(j, RIGHT)
        if j in CROSS:
            pl.when(odd)(lambda: onward(j, RIGHT, ag_r.at[j, 5], peer(0, 1, 0)))
            pl.when(jnp.logical_not(odd))(lambda: onward(j, LEFT, ag_r.at[j, 4], peer(0, 1, 0)))
        arrived(j, PARTNER)
        if j in CROSS:
            pl.when(odd)(lambda: onward(j, PARTNER, ag_r.at[j, 5], peer(3, 0, 0)))
            pl.when(jnp.logical_not(odd))(lambda: onward(j, PARTNER, ag_r.at[j, 4], peer(1, 0, 0)))
        else:
            onward(j, PARTNER, ag_r.at[j, 4], peer(1, 0, 0))
            onward(j, PARTNER, ag_r.at[j, 5], peer(3, 0, 0))
        across(j, PARTNER)

    def far(j):
        arrived(j, FAR)
        onward(j, FAR, ag_r.at[j, 6], peer(0, 1, 0))
        across(j, FAR)

    def last(j):
        for k in (4, 5, 6):
            arrived(j, k)
            across(j, k)

    def choose():
        wide = jnp.broadcast_to(dest_ref[...], (TILE, TILE)).astype(F32)
        earlier = lax.broadcasted_iota(jnp.int32, (TILE, TILE), 0) < lax.broadcasted_iota(jnp.int32, (TILE, TILE), 1)
        same = jnp.where(earlier & (wide == wide.T), 1.0, 0.0)
        place = dest_ref[...].astype(F32) * SLOTS + jnp.sum(same, axis=0, keepdims=True)
        slot = lax.broadcasted_iota(jnp.int32, pick_ref.shape, 0).astype(F32)
        pick_ref[...] = jnp.where(slot == place, 1.0, 0.0).astype(BF16)

    def picked(part):
        high = jnp.floor(part * (1.0 / 256.0))
        moved = 256.0 * dot(pick_ref[...], high.astype(BF16)) + dot(pick_ref[...], (part - high * 256.0).astype(BF16))
        return moved.reshape(16, SLOTS, part.shape[1])

    def flag(t):
        return flags[0, t].astype(F32)

    def fill(j):
        start = sum(SPANS[:j])

        def block(i, _):
            s = pl.ds(pl.multiple_of(start + i * BLOCK, BLOCK), BLOCK)
            first = start // TILE + i * (BLOCK // TILE)
            mask = jnp.concatenate([jnp.full((1, TILE), flag(first + t), F32) for t in range(BLOCK // TILE)], axis=1)
            rows[:, :, s] = picked(thin[:, s] * mask)
            return 0

        lax.fori_loop(0, SPANS[j] // BLOCK, block, 0)

    def rows_out(j):
        s = columns(j)
        for off in OTHERS:
            to = peer(*off)
            send(rows.at[to, :, s], g.at[r, :, s], row_s.at[j], row_r.at[j], to).start()
        pltpu.make_async_copy(rows.at[r, :, s], g.at[r, :, s], row_l.at[j]).start()

    def tile_along(k):
        there = lax.rem(y + k, 4)
        return send(tile.at[lax.rem(there, 2)], tile_in.at[k], tile_s.at[k], tile_r.at[k], r, along_y(k))

    def tile_across():
        return send(tile_sum, tile_in.at[0], tile_s.at[0], tile_r.at[0], r, across_z)

    def select():
        def one(t, found):
            s = pl.ds(pl.multiple_of(t * TILE, TILE), TILE)
            part, head = thin[:, s], piv_ref[pl.ds(0, 8), s]
            at = [jnp.where(wanted[k] == c * flags.shape[1] + t, 1.0, 0.0) for k in range(2)]
            return (
                found[0] + part * (flag(t) * at[0]),
                found[1] + part * (flag(t) * at[1]),
                found[2] + head * at[1],
            )

        none = jnp.zeros((TILE, TILE), F32)
        found = lax.fori_loop(0, flags.shape[1], one, (none, none, jnp.zeros((8, TILE), F32)))
        for k in range(2):
            tile[k, pl.ds(0, TILE), :] = found[k]
            tile[k, pl.ds(TILE, 8), :] = found[2]

    def tile_begin():
        for k in (1, 2, 3):
            tile_along(k).start()

    def tile_next():
        total = jnp.where(lax.rem(y, 2) == 0, tile[0], tile[1])
        for k in (1, 2, 3):
            tile_along(k).wait_recv()
            total = total + tile_in[k]
        tile_sum[...] = total
        tile_across().start()

    def ext_begin():
        tile_across().wait_recv()
        total = tile_sum[...] + tile_in[0]
        slots = picked(total[:TILE, :])
        ext_out[:, pl.ds(0, 8), :] = jnp.where(y < 2, slots[:, :8], slots[:, 8:])
        ext_out[:, pl.ds(8, 8), :] = jnp.broadcast_to(total[TILE:, :][None], (16, 8, TILE))
        for off in OTHERS:
            to = peer(*off)
            send(ext_out.at[to], ext.at[y, r], ext_s, ext_r, to).start()
        pltpu.make_async_copy(ext_out.at[r], ext.at[y, r], ext_l).start()

    def ext_along(k):
        return send(ext.at[y], ext.at[y], ext_y, ext_in, r, along_y(k))

    def ext_next():
        took(ext.at[y, pl.ds(0, 15)], ext_r)
        took(ext.at[y, 0], ext_l)
        for k in (1, 2, 3):
            ext_along(k).start()

    def keep(parts, at):
        for ref, part in zip((hi_ref, lo_ref), parts):
            ref[:, pl.ds(at, part.shape[1])] = part

    def kept(at):
        return hi_ref[:, pl.ds(at, TILE)], lo_ref[:, pl.ds(at, TILE)]

    zero = jnp.zeros((16 * SLOTS, 1), F32)

    def factors():
        took(ext.at[pl.ds(0, 3)], ext_in)
        for copy in constants:
            copy.wait()
        halves = [ext[k, :, :8, :] for k in range(4)]
        terms = [jnp.concatenate([halves[k], halves[k + 2]], axis=1).reshape(16 * SLOTS, TILE) for k in range(2)]
        pivot = limbs(centred(ext[0, :, 8:, :].reshape(TILE, TILE)))
        first = limbs(-subtract_product(zero, limbs(centred(terms[0])), limbs(centred(r_ref[0]))))
        second = subtract_product(terms[1], first, pivot)
        second = limbs(-subtract_product(zero, limbs(second), limbs(centred(r_ref[1]))))
        keep(first, 0)
        keep(second, TILE)

    def quarter(k):
        return low.at[pl.ds(k * (4 * SLOTS), 4 * SLOTS)]

    def low_out(k):
        return send(low, low, low_s.at[k - 1], low_r, r, k)

    def low_over():
        return send(quarter(y), quarter(y), low_z, low_over_r, r, across_z)

    def low_along(k):
        return send(quarter(y), quarter(y), low_s.at[k - 1], low_r, r, along_y(k))

    def lower_begin():
        @pl.when(c == 0)
        def _():
            base = g[:, :, :PANEL].reshape(16 * SLOTS, PANEL)
            for k in range(2):
                part = lines[:, 8 * k : 8 * k + 8, :PANEL].reshape(TILE, PANEL)
                base = subtract_product(base, kept(k * TILE), limbs(centred(part)))
            low[...] = -subtract_product(zero, limbs(base), limbs(centred(big_ref[...])))
            for k in (1, 3, 2):
                low_out(k).start()

    def lower_next():
        @pl.when((plane == 0) & (y != 0))
        def _():
            low_out(1).wait_recv()

        @pl.when(plane == 0)
        def _():
            low_over().start()

        @pl.when(plane == 1)
        def _():
            low_over().wait_recv()
            for k in (1, 3, 2):
                low_along(k).start()

    def lower_end():
        @pl.when(plane == 1)
        def _():
            took(low.at[pl.ds(0, 12 * SLOTS)], low_r)

        keep(limbs(low[...]), 2 * TILE)

    def lines_done(j):
        took(lines.at[pl.ds(0, 8), :, columns(j)], core_r.at[j])
        took(slab(j, r), ag_l.at[j])

    def rows_done(j):
        took(g.at[pl.ds(0, 15), :, columns(j)], row_r.at[j])
        took(g.at[0, :, columns(j)], row_l.at[j])

    def each_block(j, body):
        def block(i, _):
            body(pl.multiple_of(sum(SPANS[:j]) + i * BLOCK, BLOCK))
            return 0

        lax.fori_loop(0, SPANS[j] // BLOCK, block, 0)

    def ready_at(at):
        return pl.ds(pl.multiple_of(at - sum(SPANS[:LATE]), BLOCK), BLOCK)

    def put(s, amount):
        g[:, :, s] = residue(g[:, :, s], amount)

    def compute(j, early=False):
        def body(at):
            s = pl.ds(at, BLOCK)
            held = lines[:, :, s]
            inner = jnp.concatenate(
                [held[:, 0:8].reshape(TILE, BLOCK), held[:, 8:16].reshape(TILE, BLOCK),
                 held[:, 16:].reshape(PANEL, BLOCK)], axis=0
            )
            amount = product((hi_ref[...], lo_ref[...]), limbs(centred(inner)))
            if early:
                ready[:, ready_at(at)] = amount
            else:
                put(s, amount)

        each_block(j, body)

    own(0)
    own(1)
    choose()
    for j in range(GROUPS):
        thin_in(j).wait()
    select()
    tile_begin()
    fill(0)
    rows_out(0)
    near(0)
    tile_next()
    far(0)
    ext_begin()
    own(2)
    fill(1)
    rows_out(1)
    last(0)
    ext_next()
    own(3)
    fill(2)
    near(1)
    factors()
    lines_done(0)
    rows_done(0)
    lower_begin()
    rows_out(2)
    own(4)
    fill(3)
    near(2)
    far(1)
    lower_next()
    own(5)
    fill(4)
    fill(5)
    near(3)
    rows_out(3)
    far(2)
    last(1)
    lower_end()
    near(4)
    rows_out(4)
    compute(0)
    far(3)
    last(2)
    near(5)
    rows_out(5)
    lines_done(1)
    rows_done(1)
    compute(1)
    far(4)
    last(3)
    lines_done(2)
    rows_done(2)
    compute(2)
    far(5)
    last(4)
    lines_done(3)
    compute(3, early=True)
    lines_done(4)
    compute(4, early=True)
    last(5)
    lines_done(5)
    compute(5, early=True)
    rows_done(3)
    rows_done(4)
    rows_done(5)

    for j in range(GROUPS):
        took(lines.at[pl.ds(0, 15), :, columns(j)], ag_s.at[j])
        took(g.at[pl.ds(0, 15), :, columns(j)], row_s.at[j])
    took(ext.at[0, pl.ds(0, 15)], ext_s)
    took(ext.at[pl.ds(0, 3)], ext_y)
    tile_across().wait_send()
    for k in (1, 2, 3):
        tile_along(k).wait_send()

    @pl.when(c == 0)
    def _():
        for k in (1, 2, 3):
            low_out(k).wait_send()

    @pl.when(plane == 0)
    def _():
        low_over().wait_send()

    @pl.when(plane == 1)
    def _():
        for k in (1, 2, 3):
            low_along(k).wait_send()


def exchange(wanted, flags, dest, thin, piv, strip, recips, big):
    width = thin.shape[1]
    dma = pltpu.SemaphoreType.DMA
    head = (TILE + 8, TILE)
    return pl.pallas_call(
        exchange_kernel,
        in_specs=[SM, SM, VM, ANY, VM, ANY, ANY, ANY],
        out_specs=[VM, VM],
        out_shape=[
            pltpu.VMEM((16, SLOTS, width), F32),
            pltpu.VMEM((16 * SLOTS, sum(SPANS[LATE:])), F32),
        ],
        scratch_shapes=[
            pltpu.VMEM((16, LINES, width), F32),
            pltpu.VMEM((16, SLOTS, width), F32),
            pltpu.VMEM(thin.shape, F32),
            pltpu.VMEM((4, 16, SLOTS, TILE), F32),
            pltpu.VMEM((16, SLOTS, TILE), F32),
            pltpu.VMEM((2,) + head, F32),
            pltpu.VMEM(head, F32),
            pltpu.VMEM((4,) + head, F32),
            pltpu.VMEM((16 * SLOTS, PANEL), F32),
            pltpu.VMEM((16 * SLOTS, 2 * TILE + PANEL), BF16),
            pltpu.VMEM((16 * SLOTS, 2 * TILE + PANEL), BF16),
            pltpu.VMEM((16 * SLOTS, TILE), BF16),
            pltpu.VMEM(recips.shape, F32),
            pltpu.VMEM(big.shape, F32),
            dma((4,)), dma((4,)), dma((3,)), dma(()), dma(()), dma(()), dma(()), dma(()),
            dma((GROUPS,)), dma((GROUPS,)), dma(()), dma(()),
            dma((GROUPS,)), dma((GROUPS, 7)), dma((GROUPS,)),
            dma((GROUPS,)), dma((GROUPS,)), dma(()), dma((GROUPS,)), dma((2,)),
        ],
        name="exchange",
        compiler_params=pltpu.CompilerParams(
            collective_id=0, has_side_effects=True, vmem_limit_bytes=48 << 20
        ),
    )(wanted, flags, dest, thin, piv, strip, recips, big)


def local(thin, flags, tiles, pivots, recips, dest, strip, big):
    width = thin.shape[1]
    g, ready = exchange(tiles, flags, dest[None, :], thin, pivots.reshape(16, width), strip, recips, big)
    return close(g, ready).reshape(16 * SLOTS, width)


def solution(mesh):
    return jax.shard_map(
        local,
        mesh=mesh,
        in_specs=(
            P("row", "col"),
            P("row", "col"),
            P(),
            P(None, "row", "col"),
            P(),
            P("row"),
            P("row", "col"),
            P(),
        ),
        out_specs=P("row", "col"),
        check_vma=False,
    )
```
